32 devices in a mesh: groups: 2 (over y), blk: 8 (over z, core), heads: 2 (over x).
Axes of the slice: x: 2, y: 2, z: 4, core: 2. Of those that a mesh axis runs over, the one named last changes fastest.
Arguments:
- span_q: bfloat16 [1024, 5120], P(('groups', 'blk'), 'heads'), parts along dimension 0, may hold values from -12 to 12
- span_k: bfloat16 [1024, 1024], P(('groups', 'blk'), 'heads'), parts along dimension 0, may hold values from -12 to 12
- span_values: bfloat16 [1024, 1024], P(('groups', 'blk'), 'heads'), parts along dimension 0, may hold values from -6 to 6
- cached_keys: bfloat16 [1024, 1024], P(('groups', 'blk'), 'heads'), parts along dimension 0, may hold values from -6 to 6
- cached_values: bfloat16 [1024, 1024], P(('groups', 'blk'), 'heads'), parts along dimension 0, may hold values from -6 to 6
- out_weight: bfloat16 [5120, 5120], P('blk', 'heads'), may hold values from -0.5 to 0.5
- ctx_len: int32 [2], P('groups'), parts along dimension 0, may hold values from 128 to 512
- span_start: int32 [2], P('groups'), parts along dimension 0, may hold values from 512 to 1023
Outputs:
- mixed: bfloat16 [5120, 1024], P('blk', ('groups', 'heads')), parts along dimension 1
The draws below stay inside these ranges and needn't reach their ends.
There are 2 independent parts, one for each index of `groups`. The reference program is written for one: setup_inputs(seed, part) draws one part's arguments, and reference() takes and returns one part's arrays. A program takes and returns all parts, laid end to end along the dimension named above; an argument that names none is the same for every part. Nothing has to cross between parts.
All inputs are finite; a program needn't handle non-finite values.
Results may differ from the reference program's by a relative error of at most 0.014.
Values may be sent and summed in bfloat16 or wider, within the bound.
No kernel may reach another device: no remote copies, remote signals or barrier semaphores. Data moves between devices by JAX's collectives and lax.ppermute only.
A program may use at most 64 MiB of HBM per device.

```python
import math
import jax
import jax.numpy as jnp
from jax import lax

D = 5120
QUERY_HEADS = 40
KEY_VALUE_HEADS = 8
HEAD_SIZE = 128
CONTEXT_TOKENS = 512
SPAN_TOKENS = 512


def paired(key):
    base_key = jax.random.fold_in(key, 7)
    key_q, key_slice = jax.random.split(base_key, 2)
    query_rows = jnp.clip(2.0 * jax.random.normal(key_q, (SPAN_TOKENS, QUERY_HEADS * HEAD_SIZE), jnp.float32), -12.0, 12.0)
    key_entries = jnp.clip(jax.random.normal(key_slice, (SPAN_TOKENS, KEY_VALUE_HEADS * HEAD_SIZE), jnp.float32), -12.0, 12.0)
    return (query_rows, key_entries)


def draw_span_q(key, part):
    return paired(key)[0].astype(jnp.bfloat16)


def draw_span_k(key, part):
    return paired(key)[1].astype(jnp.bfloat16)


def levels(own_key, shape, pieces, smallest, high):
    def one(axis_at, shards_of):
        heights = jax.random.uniform(jax.random.fold_in(jax.random.fold_in(own_key, 6), axis_at), (shards_of,), jnp.float32, smallest / len(pieces), high / len(pieces))
        return jnp.repeat(jnp.exp(heights), shape[axis_at] // shards_of).reshape((-1,) + (1,) * (len(shape) - axis_at - 1))

    factor_of = one(*pieces[0])
    for cut in pieces[1:]:
        factor_of = factor_of * one(*cut)
    return factor_of


def gaussian(key, shape, spread, limit, cuts=(), held_as=jnp.bfloat16):
    gain = levels(key, shape, cuts, -0.22, 0.18) if cuts else 1.0
    drawn = jax.random.normal(key, shape, jnp.float32) * spread * gain
    return jnp.minimum(jnp.maximum(drawn, -limit), limit).astype(held_as)


def setup_inputs(seed: int = 0, part: int = 0) -> dict:
    splits = jax.random.split(jax.random.key(seed), 9)
    part_keys = jax.random.split(jax.random.fold_in(splits[8], part), 9)
    span_q = draw_span_q(jax.random.fold_in(jax.random.fold_in(splits[8], part), 71), part)
    span_k = draw_span_k(jax.random.fold_in(jax.random.fold_in(splits[8], part), 71), part)
    span_values = gaussian(part_keys[2], (SPAN_TOKENS, KEY_VALUE_HEADS * HEAD_SIZE), 1.0, 6.0, ((0, 8), (1, 2)))
    cached_keys = gaussian(part_keys[3], (CONTEXT_TOKENS, KEY_VALUE_HEADS * HEAD_SIZE), 1.0, 6.0, ((0, 8), (1, 2)))
    cached_values = gaussian(part_keys[4], (CONTEXT_TOKENS, KEY_VALUE_HEADS * HEAD_SIZE), 1.0, 6.0, ((0, 8), (1, 2)))
    out_weight = gaussian(splits[5], (D, QUERY_HEADS * HEAD_SIZE), HEAD_SIZE ** -0.5, 0.5, ((0, 8), (1, 2)))
    ctx_len = jax.random.randint(part_keys[6], (1,), CONTEXT_TOKENS // 4, CONTEXT_TOKENS + 1).astype(jnp.int32)
    span_start = jax.random.randint(part_keys[7], (1,), CONTEXT_TOKENS, 2 * CONTEXT_TOKENS).astype(jnp.int32)
    return dict(span_q=span_q, span_k=span_k, span_values=span_values, cached_keys=cached_keys, cached_values=cached_values, out_weight=out_weight, ctx_len=ctx_len, span_start=span_start)


ROPE_BASE = 1000000.0
NEG_FILL = -1e+30

def rotary(inputs, positions):
    row_count = inputs.shape[0]
    head_count = inputs.shape[1] // HEAD_SIZE
    floats = inputs.astype(jnp.float32).reshape(row_count, head_count, HEAD_SIZE)
    half_dim = HEAD_SIZE // 2
    inverse = ROPE_BASE ** (-(jnp.arange(half_dim, dtype=jnp.float32) * 2.0 / HEAD_SIZE))
    angles = positions.astype(jnp.float32)[:, None] * inverse[None, :]
    cosine = jnp.cos(angles)[:, None, :]
    sine_val = jnp.sin(angles)[:, None, :]
    first_half = floats[..., :half_dim]
    second_half = floats[..., half_dim:]
    rotated = jnp.concatenate([first_half * cosine - second_half * sine_val, second_half * cosine + first_half * sine_val], axis=-1)
    return rotated.reshape(row_count, head_count * HEAD_SIZE).astype(jnp.bfloat16)

def reference(span_q, span_k, span_values, cached_keys, cached_values, out_weight, ctx_len, span_start):
    query_index = jnp.arange(SPAN_TOKENS, dtype=jnp.int32)
    positions = span_start[0] + query_index
    rotated_queries = rotary(span_q, positions)
    rotated_keys = rotary(span_k, positions)
    queries_per_group = QUERY_HEADS // KEY_VALUE_HEADS
    key_row_list = jnp.concatenate([cached_keys, rotated_keys], axis=0).reshape(CONTEXT_TOKENS + SPAN_TOKENS, KEY_VALUE_HEADS, HEAD_SIZE)
    value_row_list = jnp.concatenate([cached_values, span_values], axis=0).reshape(CONTEXT_TOKENS + SPAN_TOKENS, KEY_VALUE_HEADS, HEAD_SIZE)
    query_rows = rotated_queries.reshape(SPAN_TOKENS, KEY_VALUE_HEADS, queries_per_group, HEAD_SIZE)
    cached_ok = jnp.arange(CONTEXT_TOKENS, dtype=jnp.int32) < ctx_len[0]
    causal = query_index[None, :] <= query_index[:, None]
    visible = jnp.concatenate([jnp.broadcast_to(cached_ok[None, :], (SPAN_TOKENS, CONTEXT_TOKENS)), causal], axis=1)

    def one_group(stacked):
        query_set, key_set, value_set = stacked
        scores = jnp.einsum('qkd,td->kqt', query_set.astype(jnp.float32), key_set.astype(jnp.float32)) / math.sqrt(HEAD_SIZE)
        scores = jnp.where(visible[None], scores, NEG_FILL)
        largest = lax.optimization_barrier(jnp.max(scores, axis=-1, keepdims=True))
        exp_scores = jnp.exp(scores - largest)
        total = lax.optimization_barrier(jnp.sum(exp_scores, axis=-1))
        weights = exp_scores.astype(jnp.bfloat16)
        summed = jnp.einsum('kqt,td->qkd', weights.astype(jnp.float32), value_set.astype(jnp.float32))
        return (summed / jnp.transpose(total)[:, :, None]).astype(jnp.bfloat16)
    stacked = (jnp.transpose(query_rows, (1, 0, 2, 3)), jnp.transpose(key_row_list, (1, 0, 2)), jnp.transpose(value_row_list, (1, 0, 2)))
    grouped = lax.map(one_group, stacked)
    attended = jnp.transpose(grouped, (1, 0, 2, 3)).reshape(SPAN_TOKENS, QUERY_HEADS * HEAD_SIZE)
    projected = lax.dot_general(out_weight, attended, (((1,), (1,)), ((), ())), preferred_element_type=jnp.float32)
    return projected.astype(jnp.bfloat16)
```

```python
import functools
import math

import jax
import jax.numpy as jnp
from jax import lax
from jax.experimental import pallas as pl
from jax.experimental.pallas import tpu as pltpu
from jax.sharding import PartitionSpec as P

HEAD_SIZE = 128
CORES = 2


ROPE_BASE = 1000000.0
NEG_FILL = -1e30


def whole(space=pltpu.VMEM):
    return pl.BlockSpec(memory_space=space)


def pack_kernel(q_ref, k_ref, v_ref, ck_ref, cv_ref, *out_refs):
    chip = lax.axis_index("blk") // CORES
    chips = len(out_refs)
    width = q_ref.shape[1] // chips
    group = width // HEAD_SIZE
    for j, out in enumerate(out_refs):
        target = chip ^ j
        for h in range(group):
            out[h] = q_ref[:, pl.ds(pl.multiple_of(target * width + h * HEAD_SIZE, HEAD_SIZE), HEAD_SIZE)]
        for n, ref in enumerate((k_ref, v_ref, ck_ref, cv_ref)):
            out[group + n] = ref[:, pl.ds(pl.multiple_of(target * HEAD_SIZE, HEAD_SIZE), HEAD_SIZE)]


def attend_kernel(group, blocks, *refs):
    slabs = (len(refs) - 9) // 2
    own, other = refs[:slabs], refs[slabs : 2 * slabs]
    cos_ref, sin_ref, ctx_ref, out_ref, q_s, k_s, v_s, ck_s, cv_s = refs[2 * slabs :]
    me = lax.axis_index("blk")
    chip, core = me // CORES, me % CORES
    rows = own[0].shape[1]
    span = rows * CORES

    def rotate(x, start):
        x = x.astype(jnp.float32)
        turned = pltpu.roll(x, HEAD_SIZE // 2, 1)
        return (x * cos_ref[pl.ds(start, rows)] + turned * sin_ref[pl.ds(start, rows)]).astype(jnp.bfloat16)

    for j in range(slabs):
        source = chip ^ j
        for piece, side in ((own[j], core), (other[j], 1 - core)):
            at = pl.multiple_of(source * span + side * rows, rows)
            k_s[pl.ds(at, rows)] = rotate(piece[group], at)
            v_s[pl.ds(at, rows)] = piece[group + 1]
            ck_s[pl.ds(at, rows)] = piece[group + 2]
            cv_s[pl.ds(at, rows)] = piece[group + 3]
        start = pl.multiple_of(source * span + core * rows, rows)
        for h in range(group):
            at = pl.multiple_of((source * group + h) * rows, rows)
            q_s[pl.ds(at, rows)] = rotate(own[j][h], start)

    scale = 1.0 / math.sqrt(HEAD_SIZE)
    height = group * rows
    total_rows = slabs * span
    cached_ok = lax.broadcasted_iota(jnp.int32, (1, total_rows), 1) < ctx_ref[0]
    cached_bias = jnp.where(cached_ok, 0.0, NEG_FILL).astype(jnp.float32)
    row = lax.broadcasted_iota(jnp.int32, (height, span), 0) % rows + core * rows
    col = lax.broadcasted_iota(jnp.int32, (height, span), 1)
    diagonal = col <= row
    contract_last = (((1,), (1,)), ((), ()))
    for n, block in enumerate(blocks):
        q = q_s[block * height : (block + 1) * height]
        cached = lax.dot_general(q, ck_s[...], contract_last, preferred_element_type=jnp.float32)
        cached = cached * scale + cached_bias
        top = jnp.max(cached, axis=1, keepdims=True)
        parts = [(cached, cv_s[...])]
        if block:
            past = lax.dot_general(
                q, k_s[: block * span], contract_last, preferred_element_type=jnp.float32
            ) * scale
            top = jnp.maximum(top, jnp.max(past, axis=1, keepdims=True))
            parts.append((past, v_s[: block * span]))
        near = lax.dot_general(
            q, k_s[block * span : (block + 1) * span], contract_last, preferred_element_type=jnp.float32
        ) * scale
        near = jnp.where(diagonal, near, NEG_FILL)
        top = jnp.maximum(top, jnp.max(near, axis=1, keepdims=True))
        parts.append((near, v_s[block * span : (block + 1) * span]))
        total = None
        summed = None
        for scores, values in parts:
            exp_scores = jnp.exp(scores - top)
            part_total = jnp.sum(exp_scores, axis=1, keepdims=True)
            part = jnp.dot(exp_scores.astype(jnp.bfloat16), values, preferred_element_type=jnp.float32)
            total = part_total if total is None else total + part_total
            summed = part if summed is None else summed + part
        result = (summed / total).astype(jnp.bfloat16)
        for h in range(group):
            out_ref[n, :, h * HEAD_SIZE : (h + 1) * HEAD_SIZE] = result[h * rows : (h + 1) * rows]


def project_kernel(w_ref, *refs):
    pieces = (len(refs) - 3) // 2
    own, other = refs[:pieces], refs[pieces : 2 * pieces]
    send_ref, keep_ref, rows_s = refs[2 * pieces :]
    me = lax.axis_index("blk")
    chip, core = me // CORES, me % CORES
    half = lax.axis_index("heads")
    rows, width = own[0].shape[1:]
    for j in range(pieces):
        at = pl.multiple_of((chip ^ j) * width, HEAD_SIZE)
        for piece, side in ((own[j], core), (other[j], 1 - core)):
            for slot, which in ((0, 1 - half), (1, half)):
                to = pl.multiple_of((slot * CORES + side) * rows, rows)
                rows_s[pl.ds(to, rows), pl.ds(at, width)] = piece[which]
    product = lax.dot_general(
        w_ref[...], rows_s[...], (((1,), (1,)), ((), ())), preferred_element_type=jnp.float32
    )
    count = rows * CORES
    send_ref[...] = product[:, :count].astype(jnp.bfloat16)
    keep_ref[...] = product[:, count:]


def head_sharded(chips, span_q, span_k, span_values, cached_keys, cached_values, out_weight, ctx_len, span_start):
    rows = span_q.shape[0]
    group = span_q.shape[1] // span_k.shape[1]
    features = out_weight.shape[0]
    devices = chips * CORES
    total_rows = devices * rows
    width = group * HEAD_SIZE

    def along(j):
        return [(b, b ^ (CORES * j)) for b in range(devices)]

    partner = [(b, b ^ 1) for b in range(devices)]
    across = [(0, 1), (1, 0)]

    slab = jax.ShapeDtypeStruct((group + 4, rows, HEAD_SIZE), jnp.bfloat16)
    packed = pl.pallas_call(
        pack_kernel,
        out_shape=[slab] * chips,
        in_specs=[whole()] * 5,
        out_specs=[whole()] * chips,
        name="pack",
    )(span_q, span_k, span_values, cached_keys, cached_values)
    slabs = [packed[0]] + [lax.ppermute(packed[j], "blk", along(j)) for j in range(1, chips)]
    swapped = [lax.ppermute(s, "blk", partner) for s in slabs]

    half_dim = HEAD_SIZE // 2
    inverse = ROPE_BASE ** (-(jnp.arange(half_dim, dtype=jnp.float32) * 2.0 / HEAD_SIZE))
    positions = span_start[0] + jnp.arange(total_rows, dtype=jnp.int32)
    angles = positions.astype(jnp.float32)[:, None] * inverse[None, :]
    cosine, sine = jnp.cos(angles), jnp.sin(angles)
    cosine = jnp.concatenate([cosine, cosine], axis=1)
    sine = jnp.concatenate([-sine, sine], axis=1)

    chunks = (tuple(range(0, chips, 2)), tuple(range(1, chips, 2)))
    outs = []
    for blocks in chunks:
        attended = pl.pallas_call(
            functools.partial(attend_kernel, group, blocks),
            out_shape=jax.ShapeDtypeStruct((len(blocks), rows, width), jnp.bfloat16),
            in_specs=[whole()] * (2 * chips + 2) + [whole(pltpu.SMEM)],
            out_specs=whole(),
            scratch_shapes=[pltpu.VMEM((chips * group * rows, HEAD_SIZE), jnp.bfloat16)]
            + [pltpu.VMEM((total_rows, HEAD_SIZE), jnp.bfloat16)] * 4,
            name="attend",
            cost_estimate=pl.CostEstimate(flops=400_000_000, bytes_accessed=1_000_000, transcendentals=600_000),
        )(*slabs, *swapped, cosine, sine, ctx_len)
        pieces = [attended] + [lax.ppermute(attended, "blk", along(j)) for j in range(1, chips)]
        others = [lax.ppermute(p, "blk", partner) for p in pieces]
        send, keep = pl.pallas_call(
            project_kernel,
            out_shape=[
                jax.ShapeDtypeStruct((features, CORES * rows), jnp.bfloat16),
                jax.ShapeDtypeStruct((features, CORES * rows), jnp.float32),
            ],
            in_specs=[whole()] * (2 * chips + 1),
            out_specs=[whole()] * 2,
            scratch_shapes=[pltpu.VMEM((2 * CORES * rows, chips * width), jnp.bfloat16)],
            name="project",
            cost_estimate=pl.CostEstimate(flops=840_000_000, bytes_accessed=2_000_000, transcendentals=0),
        )(out_weight, *pieces, *others)
        received = lax.ppermute(send, "heads", across)
        outs.append((keep + received.astype(jnp.float32)).astype(jnp.bfloat16))
    return jnp.concatenate(outs, axis=1)


def rotary(inputs, positions):
    row_count = inputs.shape[0]
    head_count = inputs.shape[1] // HEAD_SIZE
    floats = inputs.astype(jnp.float32).reshape(row_count, head_count, HEAD_SIZE)
    half_dim = HEAD_SIZE // 2
    inverse = ROPE_BASE ** (-(jnp.arange(half_dim, dtype=jnp.float32) * 2.0 / HEAD_SIZE))
    angles = positions.astype(jnp.float32)[:, None] * inverse[None, :]
    cosine = jnp.cos(angles)[:, None, :]
    sine_val = jnp.sin(angles)[:, None, :]
    first_half = floats[..., :half_dim]
    second_half = floats[..., half_dim:]
    rotated = jnp.concatenate(
        [
            first_half * cosine - second_half * sine_val,
            second_half * cosine + first_half * sine_val,
        ],
        axis=-1,
    )
    return rotated.reshape(row_count, head_count * HEAD_SIZE).astype(jnp.bfloat16)


def token_sharded(span_q, span_k, span_values, cached_keys, cached_values, out_weight, ctx_len, span_start):
    own_index = lax.axis_index("blk")
    local_rows = span_q.shape[0]
    stored_rows = cached_keys.shape[0]
    key_heads = span_k.shape[1] // HEAD_SIZE
    queries_per_group = span_q.shape[1] // span_k.shape[1]
    query_index = own_index * local_rows + jnp.arange(local_rows, dtype=jnp.int32)
    positions = span_start[0] + query_index
    query_rows = rotary(span_q, positions).reshape(
        local_rows, key_heads, queries_per_group, HEAD_SIZE
    )
    new_keys = rotary(span_k, positions)
    cache_limit = ctx_len[0]
    initial = (
        jnp.full((key_heads, queries_per_group, local_rows), NEG_FILL, jnp.float32),
        jnp.zeros((key_heads, queries_per_group, local_rows), jnp.float32),
        jnp.zeros((key_heads, queries_per_group, local_rows, HEAD_SIZE), jnp.float32),
    )
    packed = jnp.concatenate(
        [
            jnp.concatenate([cached_keys, cached_values], axis=1),
            jnp.concatenate([new_keys, span_values], axis=1),
        ],
        axis=0,
    )
    shard_len = stored_rows + local_rows
    key_width = key_heads * HEAD_SIZE
    block_limit = 2560
    running = initial
    piece = lax.all_gather(packed, "blk", axis=0, tiled=True)
    start = jnp.int32(0)
    total_rows = piece.shape[0]
    for row_offset in range(0, total_rows, block_limit):
        row_block = piece[row_offset : row_offset + block_limit]
        row_index = start + row_offset + jnp.arange(row_block.shape[0], dtype=jnp.int32)
        shard_id = row_index // shard_len
        within = row_index % shard_len
        is_cache = within < stored_rows
        cache_pos = shard_id * stored_rows + within
        span_pos = shard_id * local_rows + within - stored_rows
        visible = jnp.where(
            is_cache[None, :],
            (cache_pos < cache_limit)[None, :],
            span_pos[None, :] <= query_index[:, None],
        )
        key_block = row_block[:, :key_width].reshape(-1, key_heads, HEAD_SIZE)
        value_block = row_block[:, key_width:].reshape(-1, key_heads, HEAD_SIZE)
        scores = jnp.einsum(
            "qgkd,tgd->gkqt", query_rows, key_block, preferred_element_type=jnp.float32
        ) / math.sqrt(HEAD_SIZE)
        scores = jnp.where(visible[None, None], scores, NEG_FILL)
        attend_largest, attend_denominator, attend_weighted = running
        new_largest = jnp.maximum(attend_largest, jnp.max(scores, axis=-1))
        shrink = jnp.exp(attend_largest - new_largest)
        exp_scores = jnp.exp(scores - new_largest[..., None])
        attend_denominator = attend_denominator * shrink + jnp.sum(exp_scores, axis=-1)
        product = jnp.einsum(
            "gkqt,tgd->gkqd",
            exp_scores.astype(jnp.bfloat16),
            value_block,
            preferred_element_type=jnp.float32,
        )
        attend_weighted = attend_weighted * shrink[..., None] + product
        running = (new_largest, attend_denominator, attend_weighted)
    largest, denominator, weighted = running
    normalized = weighted / denominator[..., None]
    attended = (
        jnp.transpose(normalized, (2, 0, 1, 3))
        .reshape(local_rows, key_heads * queries_per_group * HEAD_SIZE)
        .astype(jnp.bfloat16)
    )
    partial_value = lax.dot_general(
        out_weight,
        lax.all_gather(attended, "blk", axis=0, tiled=True),
        (((1,), (1,)), ((), ())),
        preferred_element_type=jnp.float32,
    )
    summed = lax.psum_scatter(
        partial_value.astype(jnp.bfloat16), "heads", scatter_dimension=1, tiled=True
    )
    return summed


def local(blk, heads, span_q, span_k, *others):
    chips = blk // CORES
    key_heads = span_k.shape[1] // HEAD_SIZE
    if blk == CORES * chips and key_heads == chips == 4 and heads == 2:
        return head_sharded(chips, span_q, span_k, *others)
    return token_sharded(span_q, span_k, *others)


def solution(mesh):
    placed = (
        P(("groups", "blk"), "heads"),
        P(("groups", "blk"), "heads"),
        P(("groups", "blk"), "heads"),
        P(("groups", "blk"), "heads"),
        P(("groups", "blk"), "heads"),
        P("blk", "heads"),
        P("groups"),
        P("groups"),
    )
    return jax.shard_map(
        functools.partial(local, mesh.shape["blk"], mesh.shape["heads"]),
        mesh=mesh,
        in_specs=placed,
        out_specs=P("blk", ("groups", "heads")),
        check_vma=False,
    )
```

```python
import functools
import math

import jax
import jax.numpy as jnp
from jax import lax
from jax.experimental import pallas as pl
from jax.experimental.pallas import tpu as pltpu
from jax.sharding import PartitionSpec as P


HEAD_SIZE = 128
CORES = 2


ROPE_BASE = 1000000.0
NEG_FILL = -1e30


def whole(space=pltpu.VMEM):
    return pl.BlockSpec(memory_space=space)


def room(mib):
    return pltpu.CompilerParams(vmem_limit_bytes=mib * 1024 * 1024)


def pack_kernel(chips, q_ref, k_ref, v_ref, ck_ref, cv_ref, *refs):
    outs, (held, in_sem, out_sem) = refs[:chips], refs[chips:]
    chip = lax.axis_index("blk") // CORES
    width = q_ref.shape[1] // chips
    order = list(reversed(range(chips)))
    taken, given = {}, []
    for j in order:
        target = chip ^ j
        parts = [(q_ref, target * width, 0, width)]
        for n, ref in enumerate((k_ref, v_ref, ck_ref, cv_ref)):
            parts.append((ref, target * HEAD_SIZE, width + n * HEAD_SIZE, HEAD_SIZE))
        taken[j] = [
            pltpu.make_async_copy(
                ref.at[:, pl.ds(pl.multiple_of(at, HEAD_SIZE), count)],
                held.at[j, :, pl.ds(to, count)],
                in_sem.at[j, n],
            )
            for n, (ref, at, to, count) in enumerate(parts)
        ]
        for copy in taken[j]:
            copy.start()
    for j in order:
        for copy in taken[j]:
            copy.wait()
        given.append(pltpu.make_async_copy(held.at[j], outs[j], out_sem.at[j]))
        given[-1].start()
    for copy in given:
        copy.wait()


def keep_kernel(in_ref, out_ref):
    out_ref[...] = in_ref[...]


def attend_kernel(group, blocks, *refs):
    slabs = (len(refs) - 9) // 2
    own, other = refs[:slabs], refs[slabs : 2 * slabs]
    cos_ref, sin_ref, ctx_ref, out_ref, q_s, k_s, v_s, ck_s, cv_s = refs[2 * slabs :]
    me = lax.axis_index("blk")
    chip, core = me // CORES, me % CORES
    rows = own[0].shape[0]
    span = rows * CORES

    def lanes(piece, n):
        return piece[:, n * HEAD_SIZE : (n + 1) * HEAD_SIZE]

    def rotate(x, start):
        x = x.astype(jnp.float32)
        turned = pltpu.roll(x, HEAD_SIZE // 2, 1)
        return (x * cos_ref[pl.ds(start, rows)] + turned * sin_ref[pl.ds(start, rows)]).astype(jnp.bfloat16)

    for j in range(slabs):
        source = chip ^ j
        for piece, side in ((own[j], core), (other[j], 1 - core)):
            at = pl.multiple_of(source * span + side * rows, rows)
            k_s[pl.ds(at, rows)] = rotate(lanes(piece, group), at)
            v_s[pl.ds(at, rows)] = lanes(piece, group + 1)
            ck_s[pl.ds(at, rows)] = lanes(piece, group + 2)
            cv_s[pl.ds(at, rows)] = lanes(piece, group + 3)
        start = pl.multiple_of(source * span + core * rows, rows)
        for h in range(group):
            at = pl.multiple_of((source * group + h) * rows, rows)
            q_s[pl.ds(at, rows)] = rotate(lanes(own[j], h), start)

    scale = 1.0 / math.sqrt(HEAD_SIZE)
    height = group * rows
    total_rows = slabs * span
    cached_ok = lax.broadcasted_iota(jnp.int32, (1, total_rows), 1) < ctx_ref[0]
    cached_bias = jnp.where(cached_ok, 0.0, NEG_FILL).astype(jnp.float32)
    row = lax.broadcasted_iota(jnp.int32, (height, span), 0) % rows + core * rows
    col = lax.broadcasted_iota(jnp.int32, (height, span), 1)
    diagonal = col <= row
    contract_last = (((1,), (1,)), ((), ()))
    for n, block in enumerate(blocks):
        q = q_s[block * height : (block + 1) * height]
        cached = lax.dot_general(q, ck_s[...], contract_last, preferred_element_type=jnp.float32)
        cached = cached * scale + cached_bias
        top = jnp.max(cached, axis=1, keepdims=True)
        parts = [(cached, cv_s[...])]
        if block:
            past = lax.dot_general(
                q, k_s[: block * span], contract_last, preferred_element_type=jnp.float32
            ) * scale
            top = jnp.maximum(top, jnp.max(past, axis=1, keepdims=True))
            parts.append((past, v_s[: block * span]))
        near = lax.dot_general(
            q, k_s[block * span : (block + 1) * span], contract_last, preferred_element_type=jnp.float32
        ) * scale
        near = jnp.where(diagonal, near, NEG_FILL)
        top = jnp.maximum(top, jnp.max(near, axis=1, keepdims=True))
        parts.append((near, v_s[block * span : (block + 1) * span]))
        total = None
        summed = None
        for scores, values in parts:
            exp_scores = jnp.exp(scores - top)
            part_total = jnp.sum(exp_scores, axis=1, keepdims=True)
            part = jnp.dot(exp_scores.astype(jnp.bfloat16), values, preferred_element_type=jnp.float32)
            total = part_total if total is None else total + part_total
            summed = part if summed is None else summed + part
        result = (summed / total).astype(jnp.bfloat16)
        for h in range(group):
            out_ref[n, :, h * HEAD_SIZE : (h + 1) * HEAD_SIZE] = result[h * rows : (h + 1) * rows]


def project_kernel(w_ref, *refs):
    pieces = (len(refs) - 3) // 2
    own, other = refs[:pieces], refs[pieces : 2 * pieces]
    send_ref, keep_ref, rows_s = refs[2 * pieces :]
    me = lax.axis_index("blk")
    chip, core = me // CORES, me % CORES
    half = lax.axis_index("heads")
    rows, width = own[0].shape[1:]
    for j in range(pieces):
        at = pl.multiple_of((chip ^ j) * width, HEAD_SIZE)
        for piece, side in ((own[j], core), (other[j], 1 - core)):
            for slot, which in ((0, 1 - half), (1, half)):
                to = pl.multiple_of((slot * CORES + side) * rows, rows)
                rows_s[pl.ds(to, rows), pl.ds(at, width)] = piece[which]
    product = lax.dot_general(
        w_ref[...], rows_s[...], (((1,), (1,)), ((), ())), preferred_element_type=jnp.float32
    )
    count = rows * CORES
    send_ref[...] = product[:, :count].astype(jnp.bfloat16)
    keep_ref[...] = product[:, count:]


def head_sharded(chips, span_q, span_k, span_values, cached_keys, cached_values, out_weight, ctx_len, span_start):
    rows = span_q.shape[0]
    group = span_q.shape[1] // span_k.shape[1]
    features = out_weight.shape[0]
    devices = chips * CORES
    total_rows = devices * rows
    width = group * HEAD_SIZE

    def along(j):
        return [(b, b ^ (CORES * j)) for b in range(devices)]

    partner = [(b, b ^ 1) for b in range(devices)]
    across = [(0, 1), (1, 0)]

    slab = (rows, (group + 4) * HEAD_SIZE)
    packed = pl.pallas_call(
        functools.partial(pack_kernel, chips),
        out_shape=[jax.ShapeDtypeStruct(slab, jnp.bfloat16)] * chips,
        in_specs=[whole(pl.ANY)] * 5,
        out_specs=[whole(pl.ANY)] * chips,
        scratch_shapes=[
            pltpu.VMEM((chips, *slab), jnp.bfloat16),
            pltpu.SemaphoreType.DMA((chips, 5)),
            pltpu.SemaphoreType.DMA((chips,)),
        ],
        name="pack",
    )(span_q, span_k, span_values, cached_keys, cached_values)
    half_dim = HEAD_SIZE // 2
    inverse = ROPE_BASE ** (-(jnp.arange(half_dim, dtype=jnp.float32) * 2.0 / HEAD_SIZE))
    positions = span_start[0] + jnp.arange(total_rows, dtype=jnp.int32)
    angles = positions.astype(jnp.float32)[:, None] * inverse[None, :]
    cosine, sine = jnp.cos(angles), jnp.sin(angles)
    cosine = jnp.concatenate([cosine, cosine], axis=1)
    sine = jnp.concatenate([-sine, sine], axis=1)

    def move(x, axis, pairs):
        return lax.ppermute(x, axis, pairs)

    third = move(packed[3], "blk", along(3))
    second = move(packed[2], "blk", along(2))
    first = move(packed[1], "blk", along(1))
    first, cosine, sine = lax.optimization_barrier((first, cosine, sine))
    own = pl.pallas_call(
        keep_kernel,
        out_shape=jax.ShapeDtypeStruct(slab, jnp.bfloat16),
        in_specs=[whole()],
        out_specs=whole(),
        name="own",
        compiler_params=room(2),
    )(packed[0])
    slabs = [own, first, second, third]
    swapped = [move(x, "blk", partner) for x in (packed[0], first, second, third)]
    attended = []
    for blocks in ((0, 2), (1, 3)):
        attended.append(
            pl.pallas_call(
                functools.partial(attend_kernel, group, blocks),
                out_shape=jax.ShapeDtypeStruct((len(blocks), rows, width), jnp.bfloat16),
                in_specs=[whole()] * (2 * chips + 2) + [whole(pltpu.SMEM)],
                out_specs=whole(),
                scratch_shapes=[pltpu.VMEM((chips * group * rows, HEAD_SIZE), jnp.bfloat16)]
                + [pltpu.VMEM((total_rows, HEAD_SIZE), jnp.bfloat16)] * 4,
                name="attend",
                compiler_params=room(12),
                cost_estimate=pl.CostEstimate(
                    flops=400_000_000, bytes_accessed=1_000_000, transcendentals=600_000
                ),
            )(*slabs, *swapped, cosine, sine, ctx_len)
        )
    halves = []
    for tag, rows_of in zip("AB", attended):
        far = move(rows_of, "blk", along(2))
        near = move(rows_of, "blk", along(1))
        relayed = move(far, "blk", along(1)) if tag == "A" else move(rows_of, "blk", along(3))
        pieces = [rows_of, near, far, relayed]
        others = [move(piece, "blk", partner) for piece in pieces]
        count = CORES * rows
        send, keep = pl.pallas_call(
            project_kernel,
            out_shape=[
                jax.ShapeDtypeStruct((features, count), jnp.bfloat16),
                jax.ShapeDtypeStruct((features, count), jnp.float32),
            ],
            in_specs=[whole()] * (1 + 2 * len(pieces)),
            out_specs=[whole()] * 2,
            scratch_shapes=[pltpu.VMEM((2 * count, chips * width), jnp.bfloat16)],
            name="project",
            compiler_params=room(12),
            cost_estimate=pl.CostEstimate(flops=840_000_000, bytes_accessed=2_000_000, transcendentals=0),
        )(out_weight, *pieces, *others)
        received = move(send, "heads", across)
        halves.append((keep + received.astype(jnp.float32)).astype(jnp.bfloat16))
    return jnp.concatenate(halves, axis=1)


def rotary(inputs, positions):
    row_count = inputs.shape[0]
    head_count = inputs.shape[1] // HEAD_SIZE
    floats = inputs.astype(jnp.float32).reshape(row_count, head_count, HEAD_SIZE)
    half_dim = HEAD_SIZE // 2
    inverse = ROPE_BASE ** (-(jnp.arange(half_dim, dtype=jnp.float32) * 2.0 / HEAD_SIZE))
    angles = positions.astype(jnp.float32)[:, None] * inverse[None, :]
    cosine = jnp.cos(angles)[:, None, :]
    sine_val = jnp.sin(angles)[:, None, :]
    first_half = floats[..., :half_dim]
    second_half = floats[..., half_dim:]
    rotated = jnp.concatenate(
        [
            first_half * cosine - second_half * sine_val,
            second_half * cosine + first_half * sine_val,
        ],
        axis=-1,
    )
    return rotated.reshape(row_count, head_count * HEAD_SIZE).astype(jnp.bfloat16)


def token_sharded(span_q, span_k, span_values, cached_keys, cached_values, out_weight, ctx_len, span_start):
    own_index = lax.axis_index("blk")
    local_rows = span_q.shape[0]
    stored_rows = cached_keys.shape[0]
    key_heads = span_k.shape[1] // HEAD_SIZE
    queries_per_group = span_q.shape[1] // span_k.shape[1]
    query_index = own_index * local_rows + jnp.arange(local_rows, dtype=jnp.int32)
    positions = span_start[0] + query_index
    query_rows = rotary(span_q, positions).reshape(
        local_rows, key_heads, queries_per_group, HEAD_SIZE
    )
    new_keys = rotary(span_k, positions)
    cache_limit = ctx_len[0]
    initial = (
        jnp.full((key_heads, queries_per_group, local_rows), NEG_FILL, jnp.float32),
        jnp.zeros((key_heads, queries_per_group, local_rows), jnp.float32),
        jnp.zeros((key_heads, queries_per_group, local_rows, HEAD_SIZE), jnp.float32),
    )
    packed = jnp.concatenate(
        [
            jnp.concatenate([cached_keys, cached_values], axis=1),
            jnp.concatenate([new_keys, span_values], axis=1),
        ],
        axis=0,
    )
    shard_len = stored_rows + local_rows
    key_width = key_heads * HEAD_SIZE
    block_limit = 2560
    running = initial
    piece = lax.all_gather(packed, "blk", axis=0, tiled=True)
    start = jnp.int32(0)
    total_rows = piece.shape[0]
    for row_offset in range(0, total_rows, block_limit):
        row_block = piece[row_offset : row_offset + block_limit]
        row_index = start + row_offset + jnp.arange(row_block.shape[0], dtype=jnp.int32)
        shard_id = row_index // shard_len
        within = row_index % shard_len
        is_cache = within < stored_rows
        cache_pos = shard_id * stored_rows + within
        span_pos = shard_id * local_rows + within - stored_rows
        visible = jnp.where(
            is_cache[None, :],
            (cache_pos < cache_limit)[None, :],
            span_pos[None, :] <= query_index[:, None],
        )
        key_block = row_block[:, :key_width].reshape(-1, key_heads, HEAD_SIZE)
        value_block = row_block[:, key_width:].reshape(-1, key_heads, HEAD_SIZE)
        scores = jnp.einsum(
            "qgkd,tgd->gkqt", query_rows, key_block, preferred_element_type=jnp.float32
        ) / math.sqrt(HEAD_SIZE)
        scores = jnp.where(visible[None, None], scores, NEG_FILL)
        attend_largest, attend_denominator, attend_weighted = running
        new_largest = jnp.maximum(attend_largest, jnp.max(scores, axis=-1))
        shrink = jnp.exp(attend_largest - new_largest)
        exp_scores = jnp.exp(scores - new_largest[..., None])
        attend_denominator = attend_denominator * shrink + jnp.sum(exp_scores, axis=-1)
        product = jnp.einsum(
            "gkqt,tgd->gkqd",
            exp_scores.astype(jnp.bfloat16),
            value_block,
            preferred_element_type=jnp.float32,
        )
        attend_weighted = attend_weighted * shrink[..., None] + product
        running = (new_largest, attend_denominator, attend_weighted)
    _, denominator, weighted = running
    normalized = weighted / denominator[..., None]
    attended = (
        jnp.transpose(normalized, (2, 0, 1, 3))
        .reshape(local_rows, key_heads * queries_per_group * HEAD_SIZE)
        .astype(jnp.bfloat16)
    )
    partial_value = lax.dot_general(
        out_weight,
        lax.all_gather(attended, "blk", axis=0, tiled=True),
        (((1,), (1,)), ((), ())),
        preferred_element_type=jnp.float32,
    )
    summed = lax.psum_scatter(
        partial_value.astype(jnp.bfloat16), "heads", scatter_dimension=1, tiled=True
    )
    return summed


def local(blk, heads, span_q, span_k, *others):
    chips = blk // CORES
    key_heads = span_k.shape[1] // HEAD_SIZE
    if by_head(blk, heads, key_heads):
        return head_sharded(chips, span_q, span_k, *others)
    return token_sharded(span_q, span_k, *others)


def by_head(blk, heads, key_heads):
    return blk == CORES * key_heads and key_heads == 4 and heads == 2


def solution(mesh):
    placed = (
        P(("groups", "blk"), "heads"),
        P(("groups", "blk"), "heads"),
        P(("groups", "blk"), "heads"),
        P(("groups", "blk"), "heads"),
        P(("groups", "blk"), "heads"),
        P("blk", "heads"),
        P("groups"),
        P("groups"),
    )
    return jax.shard_map(
        functools.partial(local, mesh.shape["blk"], mesh.shape["heads"]),
        mesh=mesh,
        in_specs=placed,
        out_specs=P("blk", ("groups", "heads")),
        check_vma=False,
    )
```

```python
import functools
import math

import jax
import jax.numpy as jnp
import numpy as np
from jax import lax
from jax.experimental import pallas as pl
from jax.experimental.pallas import tpu as pltpu
from jax.sharding import PartitionSpec as P


HEAD_SIZE = 128
CORES = 2


ROPE_BASE = 1000000.0
NEG_FILL = -1e30


def whole(space=pltpu.VMEM):
    return pl.BlockSpec(memory_space=space)


def room(mib):
    return pltpu.CompilerParams(vmem_limit_bytes=mib * 1024 * 1024)


def pack_kernel(chips, groups, *refs):
    total = sum(groups)
    arrays, refs = refs[:total], refs[total:]
    chip = lax.axis_index("blk") // CORES
    order = list(reversed(range(chips)))
    taken, given = {}, []
    for g, size in enumerate(groups):
        outs, held, in_sem = refs[g * chips : (g + 1) * chips], refs[g - 3 * len(groups)], refs[g - 2 * len(groups)]
        for j in order:
            taken[g, j] = []
            to = 0
            for n, ref in enumerate(arrays[sum(groups[:g]) : sum(groups[:g]) + size]):
                count = ref.shape[1] // chips
                at = pl.multiple_of((chip ^ j) * count, HEAD_SIZE)
                taken[g, j].append(
                    pltpu.make_async_copy(
                        ref.at[:, pl.ds(at, count)], held.at[j, :, pl.ds(to, count)], in_sem.at[j, n]
                    )
                )
                taken[g, j][-1].start()
                to += count
    for g in range(len(groups)):
        outs, held, out_sem = refs[g * chips : (g + 1) * chips], refs[g - 3 * len(groups)], refs[g - len(groups)]
        for j in order:
            for copy in taken[g, j]:
                copy.wait()
            given.append(pltpu.make_async_copy(held.at[j], outs[j], out_sem.at[j]))
            given[-1].start()
    for copy in given:
        copy.wait()


def pack(chips, *groups):
    slabs = [(group[0].shape[0], sum(x.shape[1] for x in group) // chips) for group in groups]
    out = pl.pallas_call(
        functools.partial(pack_kernel, chips, [len(group) for group in groups]),
        out_shape=[jax.ShapeDtypeStruct(slab, jnp.bfloat16) for slab in slabs for _ in range(chips)],
        in_specs=[whole(pl.ANY) for group in groups for _ in group],
        out_specs=[whole(pl.ANY) for _ in slabs for _ in range(chips)],
        scratch_shapes=[pltpu.VMEM((chips, *slab), jnp.bfloat16) for slab in slabs]
        + [pltpu.SemaphoreType.DMA((chips, len(group))) for group in groups]
        + [pltpu.SemaphoreType.DMA((chips,)) for _ in groups],
        name="pack",
    )(*(x for group in groups for x in group))
    return [out[g * chips : (g + 1) * chips] for g in range(len(groups))]


def attend_kernel(group, own_half, *refs):
    slabs = (len(refs) - 9) // 3
    queries, own, other = refs[:slabs], refs[slabs : 2 * slabs], refs[2 * slabs : 3 * slabs]
    cos_ref, sin_ref, ctx_ref, out_ref, q_s, k_s, v_s, ck_s, cv_s = refs[3 * slabs :]
    me = lax.axis_index("blk")
    chip, core = me // CORES, me % CORES
    rows = own[0].shape[0]
    span = rows * CORES

    def lanes(piece, n):
        return piece[:, n * HEAD_SIZE : (n + 1) * HEAD_SIZE]

    def rotate(x, start):
        x = x.astype(jnp.float32)
        turned = pltpu.roll(x, HEAD_SIZE // 2, 1)
        return (x * cos_ref[pl.ds(start, rows)] + turned * sin_ref[pl.ds(start, rows)]).astype(jnp.bfloat16)

    for j in range(slabs):
        source = chip ^ j
        for piece, side in ((own[j], core), (other[j], 1 - core)):
            at = pl.multiple_of(source * span + side * rows, rows)
            k_s[pl.ds(at, rows)] = rotate(lanes(piece, 0), at)
            v_s[pl.ds(at, rows)] = lanes(piece, 1)
            ck_s[pl.ds(at, rows)] = lanes(piece, 2)
            cv_s[pl.ds(at, rows)] = lanes(piece, 3)
        start = pl.multiple_of(source * span + core * rows, rows)
        for h in range(group):
            at = pl.multiple_of((source * group + h) * rows, rows)
            q_s[pl.ds(at, rows)] = rotate(lanes(queries[j], h), start)

    scale = 1.0 / math.sqrt(HEAD_SIZE)
    height = group * rows
    total_rows = slabs * span
    cached_ok = lax.broadcasted_iota(jnp.int32, (1, total_rows), 1) < ctx_ref[0]
    cached_bias = jnp.where(cached_ok, 0.0, NEG_FILL).astype(jnp.float32)
    row = lax.broadcasted_iota(jnp.int32, (height, span), 0) % rows + core * rows
    col = lax.broadcasted_iota(jnp.int32, (height, span), 1)
    diagonal = col <= row
    contract_last = (((1,), (1,)), ((), ()))

    def attend(blocks):
        for n, block in enumerate(blocks):
            q = q_s[block * height : (block + 1) * height]
            cached = lax.dot_general(q, ck_s[...], contract_last, preferred_element_type=jnp.float32)
            cached = cached * scale + cached_bias
            top = jnp.max(cached, axis=1, keepdims=True)
            parts = [(cached, cv_s[...])]
            if block:
                past = lax.dot_general(
                    q, k_s[: block * span], contract_last, preferred_element_type=jnp.float32
                ) * scale
                top = jnp.maximum(top, jnp.max(past, axis=1, keepdims=True))
                parts.append((past, v_s[: block * span]))
            near = lax.dot_general(
                q, k_s[block * span : (block + 1) * span], contract_last, preferred_element_type=jnp.float32
            ) * scale
            near = jnp.where(diagonal, near, NEG_FILL)
            top = jnp.maximum(top, jnp.max(near, axis=1, keepdims=True))
            parts.append((near, v_s[block * span : (block + 1) * span]))
            total = None
            summed = None
            for scores, values in parts:
                exp_scores = jnp.exp(scores - top)
                part_total = jnp.sum(exp_scores, axis=1, keepdims=True)
                part = jnp.dot(exp_scores.astype(jnp.bfloat16), values, preferred_element_type=jnp.float32)
                total = part_total if total is None else total + part_total
                summed = part if summed is None else summed + part
            result = (summed / total).astype(jnp.bfloat16)
            for h in range(group):
                out_ref[n, :, h * HEAD_SIZE : (h + 1) * HEAD_SIZE] = result[h * rows : (h + 1) * rows]

    half = lax.axis_index("heads")
    for value in range(2):
        which = value if own_half else 1 - value
        blocks = tuple(range(which * slabs // 2, (which + 1) * slabs // 2))
        pl.when(half == value)(functools.partial(attend, blocks))


def project_kernel(picks, w_ref, *refs):
    pieces = len(picks)
    own, other, added = refs[:pieces], refs[pieces : 2 * pieces], refs[2 * pieces : -2]
    out_ref, rows_s = refs[-2:]
    me = lax.axis_index("blk")
    chip, core = me // CORES, me % CORES
    rows, width = own[0].shape[1:]
    for j, blocks in enumerate(picks):
        at = pl.multiple_of((chip ^ j) * width, HEAD_SIZE)
        for piece, side in ((own[j], core), (other[j], 1 - core)):
            for n, block in enumerate(blocks):
                to = pl.multiple_of((n * CORES + side) * rows, rows)
                rows_s[pl.ds(to, rows), pl.ds(at, width)] = piece[block]
    product = lax.dot_general(
        w_ref[...], rows_s[...], (((1,), (1,)), ((), ())), preferred_element_type=jnp.float32
    )
    if not added:
        out_ref[...] = product.astype(jnp.bfloat16)
    for n, ref in enumerate(added):
        count = ref.shape[1]
        lanes = slice(n * count, (n + 1) * count)
        out_ref[:, lanes] = (product[:, lanes] + ref[...].astype(jnp.float32)).astype(jnp.bfloat16)


def head_sharded(chips, span_q, span_k, span_values, cached_keys, cached_values, out_weight, ctx_len, span_start):
    rows = span_q.shape[0]
    group = span_q.shape[1] // span_k.shape[1]
    features = out_weight.shape[0]
    devices = chips * CORES
    total_rows = devices * rows
    width = group * HEAD_SIZE

    def along(j):
        return [(b, b ^ (CORES * j)) for b in range(devices)]

    partner = [(b, b ^ 1) for b in range(devices)]
    across = [(0, 1), (1, 0)]

    keyed, asked = pack(chips, (span_k, span_values, cached_keys, cached_values), (span_q,))
    half_dim = HEAD_SIZE // 2
    inverse = jnp.asarray(np.float32(ROPE_BASE) ** (-(np.arange(half_dim, dtype=np.float32) * 2.0 / HEAD_SIZE)))
    positions = span_start[0] + jnp.arange(total_rows, dtype=jnp.int32)
    angles = positions.astype(jnp.float32)[:, None] * inverse[None, :]
    cosine, sine = jnp.cos(angles), jnp.sin(angles)
    cosine = jnp.concatenate([cosine, cosine], axis=1)
    sine = jnp.concatenate([-sine, sine], axis=1)

    keys = [keyed[0]] + [lax.ppermute(keyed[j], "blk", along(j)) for j in range(1, chips)]
    queries = [asked[0]] + [lax.ppermute(asked[j], "blk", along(j)) for j in range(1, chips)]
    keys[1], cosine, sine = lax.optimization_barrier((keys[1], cosine, sine))
    swapped = [lax.ppermute(x, "blk", partner) for x in keys]
    here = ctx_len[0] >= 0
    keys[0], queries[0] = (jnp.where(here, x, jnp.zeros_like(x)) for x in (keys[0], queries[0]))
    half_chips = chips // 2

    def attend(own_half):
        return pl.pallas_call(
            functools.partial(attend_kernel, group, own_half),
            out_shape=jax.ShapeDtypeStruct((half_chips, rows, width), jnp.bfloat16),
            in_specs=[whole()] * (3 * chips + 2) + [whole(pltpu.SMEM)],
            out_specs=whole(),
            scratch_shapes=[pltpu.VMEM((chips * group * rows, HEAD_SIZE), jnp.bfloat16)]
            + [pltpu.VMEM((total_rows, HEAD_SIZE), jnp.bfloat16)] * 4,
            name="attend",
            compiler_params=room(12),
            cost_estimate=pl.CostEstimate(flops=400_000_000, bytes_accessed=1_000_000, transcendentals=600_000),
        )(*queries, *keys, *swapped, cosine, sine, ctx_len)

    def project(picks, pieces, others, *added):
        count = len(picks[0]) * CORES * rows
        return pl.pallas_call(
            functools.partial(project_kernel, picks),
            out_shape=jax.ShapeDtypeStruct((features, count), jnp.bfloat16),
            in_specs=[whole()] * (1 + 2 * len(pieces) + len(added)),
            out_specs=whole(),
            scratch_shapes=[pltpu.VMEM((count, chips * width), jnp.bfloat16)],
            name="project",
            compiler_params=room(12),
            cost_estimate=pl.CostEstimate(flops=3_000_000 * count, bytes_accessed=8_000 * count, transcendentals=0),
        )(out_weight, *pieces, *others, *added)

    sent = attend(False)
    far = lax.ppermute(sent, "blk", along(2))
    near = lax.ppermute(sent, "blk", along(1))
    pieces = [sent, near, far]
    others = [lax.ppermute(piece, "blk", partner) for piece in pieces]
    received = []
    for n in range(half_chips):
        relayed = lax.ppermute(far[n : n + 1], "blk", along(1))
        other = lax.ppermute(relayed, "blk", partner)
        picks = ((n,), (n,), (n,), (0,))
        partial = project(picks, [*pieces, relayed], [*others, other])
        received.append(lax.ppermute(partial, "heads", across))
    kept = attend(True)
    pieces = [kept] + [lax.ppermute(kept, "blk", along(j)) for j in (1, 2, 3)]
    others = [lax.ppermute(piece, "blk", partner) for piece in pieces]
    return project((tuple(range(half_chips)),) * chips, pieces, others, *received)


def rotary(inputs, positions):
    row_count = inputs.shape[0]
    head_count = inputs.shape[1] // HEAD_SIZE
    floats = inputs.astype(jnp.float32).reshape(row_count, head_count, HEAD_SIZE)
    half_dim = HEAD_SIZE // 2
    inverse = ROPE_BASE ** (-(jnp.arange(half_dim, dtype=jnp.float32) * 2.0 / HEAD_SIZE))
    angles = positions.astype(jnp.float32)[:, None] * inverse[None, :]
    cosine = jnp.cos(angles)[:, None, :]
    sine_val = jnp.sin(angles)[:, None, :]
    first_half = floats[..., :half_dim]
    second_half = floats[..., half_dim:]
    rotated = jnp.concatenate(
        [
            first_half * cosine - second_half * sine_val,
            second_half * cosine + first_half * sine_val,
        ],
        axis=-1,
    )
    return rotated.reshape(row_count, head_count * HEAD_SIZE).astype(jnp.bfloat16)


def token_sharded(span_q, span_k, span_values, cached_keys, cached_values, out_weight, ctx_len, span_start):
    own_index = lax.axis_index("blk")
    local_rows = span_q.shape[0]
    stored_rows = cached_keys.shape[0]
    key_heads = span_k.shape[1] // HEAD_SIZE
    queries_per_group = span_q.shape[1] // span_k.shape[1]
    query_index = own_index * local_rows + jnp.arange(local_rows, dtype=jnp.int32)
    positions = span_start[0] + query_index
    query_rows = rotary(span_q, positions).reshape(
        local_rows, key_heads, queries_per_group, HEAD_SIZE
    )
    new_keys = rotary(span_k, positions)
    cache_limit = ctx_len[0]
    initial = (
        jnp.full((key_heads, queries_per_group, local_rows), NEG_FILL, jnp.float32),
        jnp.zeros((key_heads, queries_per_group, local_rows), jnp.float32),
        jnp.zeros((key_heads, queries_per_group, local_rows, HEAD_SIZE), jnp.float32),
    )
    packed = jnp.concatenate(
        [
            jnp.concatenate([cached_keys, cached_values], axis=1),
            jnp.concatenate([new_keys, span_values], axis=1),
        ],
        axis=0,
    )
    shard_len = stored_rows + local_rows
    key_width = key_heads * HEAD_SIZE
    block_limit = 2560
    running = initial
    piece = lax.all_gather(packed, "blk", axis=0, tiled=True)
    start = jnp.int32(0)
    total_rows = piece.shape[0]
    for row_offset in range(0, total_rows, block_limit):
        row_block = piece[row_offset : row_offset + block_limit]
        row_index = start + row_offset + jnp.arange(row_block.shape[0], dtype=jnp.int32)
        shard_id = row_index // shard_len
        within = row_index % shard_len
        is_cache = within < stored_rows
        cache_pos = shard_id * stored_rows + within
        span_pos = shard_id * local_rows + within - stored_rows
        visible = jnp.where(
            is_cache[None, :],
            (cache_pos < cache_limit)[None, :],
            span_pos[None, :] <= query_index[:, None],
        )
        key_block = row_block[:, :key_width].reshape(-1, key_heads, HEAD_SIZE)
        value_block = row_block[:, key_width:].reshape(-1, key_heads, HEAD_SIZE)
        scores = jnp.einsum(
            "qgkd,tgd->gkqt", query_rows, key_block, preferred_element_type=jnp.float32
        ) / math.sqrt(HEAD_SIZE)
        scores = jnp.where(visible[None, None], scores, NEG_FILL)
        attend_largest, attend_denominator, attend_weighted = running
        new_largest = jnp.maximum(attend_largest, jnp.max(scores, axis=-1))
        shrink = jnp.exp(attend_largest - new_largest)
        exp_scores = jnp.exp(scores - new_largest[..., None])
        attend_denominator = attend_denominator * shrink + jnp.sum(exp_scores, axis=-1)
        product = jnp.einsum(
            "gkqt,tgd->gkqd",
            exp_scores.astype(jnp.bfloat16),
            value_block,
            preferred_element_type=jnp.float32,
        )
        attend_weighted = attend_weighted * shrink[..., None] + product
        running = (new_largest, attend_denominator, attend_weighted)
    _, denominator, weighted = running
    normalized = weighted / denominator[..., None]
    attended = (
        jnp.transpose(normalized, (2, 0, 1, 3))
        .reshape(local_rows, key_heads * queries_per_group * HEAD_SIZE)
        .astype(jnp.bfloat16)
    )
    partial_value = lax.dot_general(
        out_weight,
        lax.all_gather(attended, "blk", axis=0, tiled=True),
        (((1,), (1,)), ((), ())),
        preferred_element_type=jnp.float32,
    )
    summed = lax.psum_scatter(
        partial_value.astype(jnp.bfloat16), "heads", scatter_dimension=1, tiled=True
    )
    return summed


def local(blk, heads, span_q, span_k, *others):
    chips = blk // CORES
    key_heads = span_k.shape[1] // HEAD_SIZE
    if by_head(blk, heads, key_heads):
        return head_sharded(chips, span_q, span_k, *others)
    return token_sharded(span_q, span_k, *others)


def by_head(blk, heads, key_heads):
    return blk == CORES * key_heads and key_heads == 4 and heads == 2


def solution(mesh):
    placed = (
        P(("groups", "blk"), "heads"),
        P(("groups", "blk"), "heads"),
        P(("groups", "blk"), "heads"),
        P(("groups", "blk"), "heads"),
        P(("groups", "blk"), "heads"),
        P("blk", "heads"),
        P("groups"),
        P("groups"),
    )
    return jax.shard_map(
        functools.partial(local, mesh.shape["blk"], mesh.shape["heads"]),
        mesh=mesh,
        in_specs=placed,
        out_specs=P("blk", ("groups", "heads")),
        check_vma=False,
    )
```

```python
import functools
import math

import jax
import jax.numpy as jnp
from jax import lax
from jax.experimental import pallas as pl
from jax.experimental.pallas import tpu as pltpu
from jax.sharding import PartitionSpec as P


HEAD_SIZE = 128
CORES = 2


ROPE_BASE = 1000000.0
NEG_FILL = -1e30


def whole(space=pltpu.VMEM):
    return pl.BlockSpec(memory_space=space)


def room(mib):
    return pltpu.CompilerParams(vmem_limit_bytes=mib * 1024 * 1024)


KROOM = 54950
QROOM = 54800


def pack_kernel(chips, groups, *refs):
    total = sum(groups)
    arrays, refs = refs[:total], refs[total:]
    chip = lax.axis_index("blk") // CORES
    order = list(reversed(range(chips)))
    taken, given = {}, []
    for g, size in enumerate(groups):
        outs, held, in_sem = refs[g * chips : (g + 1) * chips], refs[g - 3 * len(groups)], refs[g - 2 * len(groups)]
        for j in order:
            taken[g, j] = []
            to = 0
            for n, ref in enumerate(arrays[sum(groups[:g]) : sum(groups[:g]) + size]):
                count = ref.shape[1] // chips
                at = pl.multiple_of((chip ^ j) * count, HEAD_SIZE)
                taken[g, j].append(
                    pltpu.make_async_copy(
                        ref.at[:, pl.ds(at, count)], held.at[j, :, pl.ds(to, count)], in_sem.at[j, n]
                    )
                )
                taken[g, j][-1].start()
                to += count
    for g in range(len(groups)):
        outs, held, out_sem = refs[g * chips : (g + 1) * chips], refs[g - 3 * len(groups)], refs[g - len(groups)]
        for j in order:
            for copy in taken[g, j]:
                copy.wait()
            given.append(pltpu.make_async_copy(held.at[j], outs[j], out_sem.at[j]))
            given[-1].start()
    for copy in given:
        copy.wait()


def pack(kib, chips, *groups):
    slabs = [(group[0].shape[0], sum(x.shape[1] for x in group) // chips) for group in groups]
    out = pl.pallas_call(
        functools.partial(pack_kernel, chips, [len(group) for group in groups]),
        out_shape=[jax.ShapeDtypeStruct(slab, jnp.bfloat16) for slab in slabs for _ in range(chips)],
        in_specs=[whole(pl.ANY) for group in groups for _ in group],
        out_specs=[whole(pl.ANY) for _ in slabs for _ in range(chips)],
        scratch_shapes=[pltpu.VMEM((chips, *slab), jnp.bfloat16) for slab in slabs]
        + [pltpu.SemaphoreType.DMA((chips, len(group))) for group in groups]
        + [pltpu.SemaphoreType.DMA((chips,)) for _ in groups],
        compiler_params=pltpu.CompilerParams(vmem_limit_bytes=kib * 1024),
    )(*(x for group in groups for x in group))
    return [out[g * chips : (g + 1) * chips] for g in range(len(groups))]


def attend_kernel(group, own_half, *refs):
    slabs = (len(refs) - 9) // 3
    queries, own, other = refs[:slabs], refs[slabs : 2 * slabs], refs[2 * slabs : 3 * slabs]
    cos_ref, sin_ref, ctx_ref, out_ref, q_s, k_s, v_s, ck_s, cv_s = refs[3 * slabs :]
    me = lax.axis_index("blk")
    chip, core = me // CORES, me % CORES
    rows = own[0].shape[0]
    span = rows * CORES

    def lanes(piece, n):
        return piece[:, n * HEAD_SIZE : (n + 1) * HEAD_SIZE]

    def rotate(x, start):
        x = x.astype(jnp.float32)
        turned = pltpu.roll(x, HEAD_SIZE // 2, 1)
        return (x * cos_ref[pl.ds(start, rows)] + turned * sin_ref[pl.ds(start, rows)]).astype(jnp.bfloat16)

    for j in range(slabs):
        source = chip ^ j
        for piece, side in ((own[j], core), (other[j], 1 - core)):
            at = pl.multiple_of(source * span + side * rows, rows)
            k_s[pl.ds(at, rows)] = rotate(lanes(piece, 0), at)
            v_s[pl.ds(at, rows)] = lanes(piece, 1)
            ck_s[pl.ds(at, rows)] = lanes(piece, 2)
            cv_s[pl.ds(at, rows)] = lanes(piece, 3)
        start = pl.multiple_of(source * span + core * rows, rows)
        for h in range(group):
            at = pl.multiple_of((source * group + h) * rows, rows)
            q_s[pl.ds(at, rows)] = rotate(lanes(queries[j], h), start)

    scale = 1.0 / math.sqrt(HEAD_SIZE)
    height = group * rows
    total_rows = slabs * span
    cached_ok = lax.broadcasted_iota(jnp.int32, (1, total_rows), 1) < ctx_ref[0]
    cached_bias = jnp.where(cached_ok, 0.0, NEG_FILL).astype(jnp.float32)
    row = lax.broadcasted_iota(jnp.int32, (height, span), 0) % rows + core * rows
    col = lax.broadcasted_iota(jnp.int32, (height, span), 1)
    diagonal = col <= row
    contract_last = (((1,), (1,)), ((), ()))

    def attend(blocks):
        for n, block in enumerate(blocks):
            q = q_s[block * height : (block + 1) * height]
            cached = lax.dot_general(q, ck_s[...], contract_last, preferred_element_type=jnp.float32)
            cached = cached * scale + cached_bias
            top = jnp.max(cached, axis=1, keepdims=True)
            parts = [(cached, cv_s[...])]
            if block:
                past = lax.dot_general(
                    q, k_s[: block * span], contract_last, preferred_element_type=jnp.float32
                ) * scale
                top = jnp.maximum(top, jnp.max(past, axis=1, keepdims=True))
                parts.append((past, v_s[: block * span]))
            near = lax.dot_general(
                q, k_s[block * span : (block + 1) * span], contract_last, preferred_element_type=jnp.float32
            ) * scale
            near = jnp.where(diagonal, near, NEG_FILL)
            top = jnp.maximum(top, jnp.max(near, axis=1, keepdims=True))
            parts.append((near, v_s[block * span : (block + 1) * span]))
            total = None
            summed = None
            for scores, values in parts:
                exp_scores = jnp.exp(scores - top)
                part_total = jnp.sum(exp_scores, axis=1, keepdims=True)
                part = jnp.dot(exp_scores.astype(jnp.bfloat16), values, preferred_element_type=jnp.float32)
                total = part_total if total is None else total + part_total
                summed = part if summed is None else summed + part
            result = (summed / total).astype(jnp.bfloat16)
            for h in range(group):
                out_ref[n, :, h * HEAD_SIZE : (h + 1) * HEAD_SIZE] = result[h * rows : (h + 1) * rows]

    half = lax.axis_index("heads")
    for value in range(2):
        which = value if own_half else 1 - value
        blocks = tuple(range(which * slabs // 2, (which + 1) * slabs // 2))
        pl.when(half == value)(functools.partial(attend, blocks))


def project_kernel(distances, final, column, w_ref, *refs):
    pieces = len(distances)
    own, other, added = refs[:pieces], refs[pieces : 2 * pieces], refs[2 * pieces :]
    added, scratch = (added[:-4], added[-4:]) if final else (added[:-2], added[-2:])
    out_ref, rows_s = scratch[:2]
    me = lax.axis_index("blk")
    chip, core = me // CORES, me % CORES
    blocks, rows, width = own[0].shape
    apart = pieces < w_ref.shape[1] // width
    for j in range(pieces):
        at = 0 if apart else pl.multiple_of((chip ^ distances[j]) * width, HEAD_SIZE)
        for piece, side in ((own[j], core), (other[j], 1 - core)):
            for n in range(blocks):
                to = pl.multiple_of((n * CORES + side) * rows, rows)
                rows_s[j if apart else 0, pl.ds(to, rows), pl.ds(at, width)] = piece[n]

    def dot(a, b):
        return lax.dot_general(a, b, (((1,), (1,)), ((), ())), preferred_element_type=jnp.float32)

    def share(lines):
        if apart:
            total = None
            for j, distance in enumerate(distances):
                at = pl.multiple_of((chip ^ distance) * width, HEAD_SIZE)
                product = dot(w_ref[lines, pl.ds(at, width)], rows_s[j])
                total = product if total is None else total + product
        else:
            total = dot(w_ref[lines], rows_s[0])
        for ref in added:
            total = total + ref[lines, column : column + total.shape[1]].astype(jnp.float32)
        return total

    features = w_ref.shape[0]
    if not final:
        out_ref[...] = share(slice(0, features)).astype(out_ref.dtype)
        return
    staged, sem = scratch[2:]
    copies = []
    for n in range(2):
        lines = slice(n * features // 2, (n + 1) * features // 2)
        staged[lines] = share(lines).astype(out_ref.dtype)
        copies.append(pltpu.make_async_copy(staged.at[lines], out_ref.at[lines], sem.at[n]))
        copies[-1].start()
    for copy in copies:
        copy.wait()


def head_sharded(chips, span_q, span_k, span_values, cached_keys, cached_values, out_weight, ctx_len, span_start):
    rows = span_q.shape[0]
    group = span_q.shape[1] // span_k.shape[1]
    features = out_weight.shape[0]
    devices = chips * CORES
    total_rows = devices * rows
    width = group * HEAD_SIZE

    def along(j):
        return [(b, b ^ (CORES * j)) for b in range(devices)]

    partner = [(b, b ^ 1) for b in range(devices)]
    across = [(0, 1), (1, 0)]

    keyed = pack(KROOM, chips, (span_k, span_values, cached_keys, cached_values))[0]
    asked = pack(QROOM, chips, (span_q,))[0]
    half_dim = HEAD_SIZE // 2
    inverse = ROPE_BASE ** (-(jnp.arange(half_dim, dtype=jnp.float32) * 2.0 / HEAD_SIZE))
    positions = span_start[0] + jnp.arange(total_rows, dtype=jnp.int32)
    angles = positions.astype(jnp.float32)[:, None] * inverse[None, :]
    cosine, sine = jnp.cos(angles), jnp.sin(angles)
    cosine = jnp.concatenate([cosine, cosine], axis=1)
    sine = jnp.concatenate([-sine, sine], axis=1)

    keys = [keyed[0]] + [lax.ppermute(keyed[j], "blk", along(j)) for j in range(1, chips)]
    queries = [asked[0]] + [lax.ppermute(asked[j], "blk", along(j)) for j in range(1, chips)]
    keys[1], cosine, sine = lax.optimization_barrier((keys[1], cosine, sine))
    keys[0], cosine, sine = lax.optimization_barrier((keys[0], cosine, sine))
    swapped = [lax.ppermute(x, "blk", partner) for x in keys]
    half_chips = chips // 2

    def attend(own_half):
        return pl.pallas_call(
            functools.partial(attend_kernel, group, own_half),
            out_shape=jax.ShapeDtypeStruct((half_chips, rows, width), jnp.bfloat16),
            in_specs=[whole()] * (3 * chips + 2) + [whole(pltpu.SMEM)],
            out_specs=whole(),
            scratch_shapes=[pltpu.VMEM((chips * group * rows, HEAD_SIZE), jnp.bfloat16)]
            + [pltpu.VMEM((total_rows, HEAD_SIZE), jnp.bfloat16)] * 4,
            name="attend",
            compiler_params=room(12),
            cost_estimate=pl.CostEstimate(flops=400_000_000, bytes_accessed=1_000_000, transcendentals=600_000),
        )(*queries, *keys, *swapped, cosine, sine, ctx_len)


    def project(distances, pieces, others, *added, dtype=jnp.bfloat16, final=False, column=0):
        count = pieces[0].shape[0] * CORES * rows
        apart = len(pieces) < chips
        scratch = [pltpu.VMEM((len(pieces), count, width) if apart else (1, count, chips * width), jnp.bfloat16)]
        if final:
            scratch += [pltpu.VMEM((features, count), dtype), pltpu.SemaphoreType.DMA((2,))]
        return pl.pallas_call(
            functools.partial(project_kernel, distances, final, column),
            out_shape=jax.ShapeDtypeStruct((features, count), dtype),
            in_specs=[whole()] * (1 + 2 * len(pieces) + len(added)),
            out_specs=whole(pl.ANY if final else pltpu.VMEM),
            scratch_shapes=scratch,
            name="project",
            compiler_params=room(12),
            cost_estimate=pl.CostEstimate(
                flops=2 * features * width * count * len(pieces), bytes_accessed=1_000_000, transcendentals=0
            ),
        )(out_weight, *pieces, *others, *added)

    def swap(pieces):
        return [lax.ppermute(piece, "blk", partner) for piece in pieces]

    sent = attend(False)
    far = lax.ppermute(sent, "blk", along(2))
    near = lax.ppermute(sent, "blk", along(1))
    pieces = [sent, near, far]
    early = project((0, 1, 2), pieces, swap(pieces), dtype=jnp.float32)
    received = []
    for n in range(half_chips):
        relayed = lax.ppermute(far[n : n + 1], "blk", along(1))
        other = lax.ppermute(relayed, "blk", partner)
        partial = project((3,), [relayed], [other], early, column=n * CORES * rows)
        received.append(lax.ppermute(partial, "heads", across))
    kept = attend(True)
    pieces = [kept] + [lax.ppermute(kept, "blk", along(j)) for j in (1, 2, 3)]
    others = swap(pieces)
    return project((0, 1, 2, 3), pieces, others, jnp.concatenate(received, axis=1), final=True)


def rotary(inputs, positions):
    row_count = inputs.shape[0]
    head_count = inputs.shape[1] // HEAD_SIZE
    floats = inputs.astype(jnp.float32).reshape(row_count, head_count, HEAD_SIZE)
    half_dim = HEAD_SIZE // 2
    inverse = ROPE_BASE ** (-(jnp.arange(half_dim, dtype=jnp.float32) * 2.0 / HEAD_SIZE))
    angles = positions.astype(jnp.float32)[:, None] * inverse[None, :]
    cosine = jnp.cos(angles)[:, None, :]
    sine_val = jnp.sin(angles)[:, None, :]
    first_half = floats[..., :half_dim]
    second_half = floats[..., half_dim:]
    rotated = jnp.concatenate(
        [
            first_half * cosine - second_half * sine_val,
            second_half * cosine + first_half * sine_val,
        ],
        axis=-1,
    )
    return rotated.reshape(row_count, head_count * HEAD_SIZE).astype(jnp.bfloat16)


def token_sharded(span_q, span_k, span_values, cached_keys, cached_values, out_weight, ctx_len, span_start):
    own_index = lax.axis_index("blk")
    local_rows = span_q.shape[0]
    stored_rows = cached_keys.shape[0]
    key_heads = span_k.shape[1] // HEAD_SIZE
    queries_per_group = span_q.shape[1] // span_k.shape[1]
    query_index = own_index * local_rows + jnp.arange(local_rows, dtype=jnp.int32)
    positions = span_start[0] + query_index
    query_rows = rotary(span_q, positions).reshape(
        local_rows, key_heads, queries_per_group, HEAD_SIZE
    )
    new_keys = rotary(span_k, positions)
    cache_limit = ctx_len[0]
    initial = (
        jnp.full((key_heads, queries_per_group, local_rows), NEG_FILL, jnp.float32),
        jnp.zeros((key_heads, queries_per_group, local_rows), jnp.float32),
        jnp.zeros((key_heads, queries_per_group, local_rows, HEAD_SIZE), jnp.float32),
    )
    packed = jnp.concatenate(
        [
            jnp.concatenate([cached_keys, cached_values], axis=1),
            jnp.concatenate([new_keys, span_values], axis=1),
        ],
        axis=0,
    )
    shard_len = stored_rows + local_rows
    key_width = key_heads * HEAD_SIZE
    block_limit = 2560
    running = initial
    piece = lax.all_gather(packed, "blk", axis=0, tiled=True)
    start = jnp.int32(0)
    total_rows = piece.shape[0]
    for row_offset in range(0, total_rows, block_limit):
        row_block = piece[row_offset : row_offset + block_limit]
        row_index = start + row_offset + jnp.arange(row_block.shape[0], dtype=jnp.int32)
        shard_id = row_index // shard_len
        within = row_index % shard_len
        is_cache = within < stored_rows
        cache_pos = shard_id * stored_rows + within
        span_pos = shard_id * local_rows + within - stored_rows
        visible = jnp.where(
            is_cache[None, :],
            (cache_pos < cache_limit)[None, :],
            span_pos[None, :] <= query_index[:, None],
        )
        key_block = row_block[:, :key_width].reshape(-1, key_heads, HEAD_SIZE)
        value_block = row_block[:, key_width:].reshape(-1, key_heads, HEAD_SIZE)
        scores = jnp.einsum(
            "qgkd,tgd->gkqt", query_rows, key_block, preferred_element_type=jnp.float32
        ) / math.sqrt(HEAD_SIZE)
        scores = jnp.where(visible[None, None], scores, NEG_FILL)
        attend_largest, attend_denominator, attend_weighted = running
        new_largest = jnp.maximum(attend_largest, jnp.max(scores, axis=-1))
        shrink = jnp.exp(attend_largest - new_largest)
        exp_scores = jnp.exp(scores - new_largest[..., None])
        attend_denominator = attend_denominator * shrink + jnp.sum(exp_scores, axis=-1)
        product = jnp.einsum(
            "gkqt,tgd->gkqd",
            exp_scores.astype(jnp.bfloat16),
            value_block,
            preferred_element_type=jnp.float32,
        )
        attend_weighted = attend_weighted * shrink[..., None] + product
        running = (new_largest, attend_denominator, attend_weighted)
    _, denominator, weighted = running
    normalized = weighted / denominator[..., None]
    attended = (
        jnp.transpose(normalized, (2, 0, 1, 3))
        .reshape(local_rows, key_heads * queries_per_group * HEAD_SIZE)
        .astype(jnp.bfloat16)
    )
    partial_value = lax.dot_general(
        out_weight,
        lax.all_gather(attended, "blk", axis=0, tiled=True),
        (((1,), (1,)), ((), ())),
        preferred_element_type=jnp.float32,
    )
    summed = lax.psum_scatter(
        partial_value.astype(jnp.bfloat16), "heads", scatter_dimension=1, tiled=True
    )
    return summed


def local(blk, heads, span_q, span_k, *others):
    chips = blk // CORES
    key_heads = span_k.shape[1] // HEAD_SIZE
    if by_head(blk, heads, key_heads):
        return head_sharded(chips, span_q, span_k, *others)
    return token_sharded(span_q, span_k, *others)


def by_head(blk, heads, key_heads):
    return blk == CORES * key_heads and key_heads == 4 and heads == 2


def solution(mesh):
    placed = (
        P(("groups", "blk"), "heads"),
        P(("groups", "blk"), "heads"),
        P(("groups", "blk"), "heads"),
        P(("groups", "blk"), "heads"),
        P(("groups", "blk"), "heads"),
        P("blk", "heads"),
        P("groups"),
        P("groups"),
    )
    return jax.shard_map(
        functools.partial(local, mesh.shape["blk"], mesh.shape["heads"]),
        mesh=mesh,
        in_specs=placed,
        out_specs=P("blk", ("groups", "heads")),
        check_vma=False,
    )
```

```python
import functools
import math

import jax
import jax.numpy as jnp
from jax import lax
from jax.experimental import pallas as pl
from jax.experimental.pallas import tpu as pltpu
from jax.sharding import PartitionSpec as P


HEAD_SIZE = 128
CORES = 2


ROPE_BASE = 1000000.0
NEG_FILL = -1e30


def whole(space=pltpu.VMEM):
    return pl.BlockSpec(memory_space=space)


def room(mib):
    return pltpu.CompilerParams(vmem_limit_bytes=mib * 1024 * 1024)


KROOM = 54950
QROOM = 54800


def pack_kernel(chips, groups, *refs):
    total = sum(groups)
    arrays, refs = refs[:total], refs[total:]
    chip = lax.axis_index("blk") // CORES
    order = list(reversed(range(chips)))
    taken, given = {}, []
    for g, size in enumerate(groups):
        outs, held, in_sem = refs[g * chips : (g + 1) * chips], refs[g - 3 * len(groups)], refs[g - 2 * len(groups)]
        for j in order:
            taken[g, j] = []
            to = 0
            for n, ref in enumerate(arrays[sum(groups[:g]) : sum(groups[:g]) + size]):
                count = ref.shape[1] // chips
                at = pl.multiple_of((chip ^ j) * count, HEAD_SIZE)
                taken[g, j].append(
                    pltpu.make_async_copy(
                        ref.at[:, pl.ds(at, count)], held.at[j, :, pl.ds(to, count)], in_sem.at[j, n]
                    )
                )
                taken[g, j][-1].start()
                to += count
    for g in range(len(groups)):
        outs, held, out_sem = refs[g * chips : (g + 1) * chips], refs[g - 3 * len(groups)], refs[g - len(groups)]
        for j in order:
            for copy in taken[g, j]:
                copy.wait()
            given.append(pltpu.make_async_copy(held.at[j], outs[j], out_sem.at[j]))
            given[-1].start()
    for copy in given:
        copy.wait()


def pack(kib, chips, *groups):
    slabs = [(group[0].shape[0], sum(x.shape[1] for x in group) // chips) for group in groups]
    out = pl.pallas_call(
        functools.partial(pack_kernel, chips, [len(group) for group in groups]),
        out_shape=[jax.ShapeDtypeStruct(slab, jnp.bfloat16) for slab in slabs for _ in range(chips)],
        in_specs=[whole(pl.ANY) for group in groups for _ in group],
        out_specs=[whole(pl.ANY) for _ in slabs for _ in range(chips)],
        scratch_shapes=[pltpu.VMEM((chips, *slab), jnp.bfloat16) for slab in slabs]
        + [pltpu.SemaphoreType.DMA((chips, len(group))) for group in groups]
        + [pltpu.SemaphoreType.DMA((chips,)) for _ in groups],
        compiler_params=pltpu.CompilerParams(vmem_limit_bytes=kib * 1024),
    )(*(x for group in groups for x in group))
    return [out[g * chips : (g + 1) * chips] for g in range(len(groups))]


def rotate(x, cosine, sine):
    x = x.astype(jnp.float32)
    turned = pltpu.roll(x, HEAD_SIZE // 2, 1)
    return (x * cosine + turned * sine).astype(jnp.bfloat16)


def lanes(piece, n):
    return piece[:, n * HEAD_SIZE : (n + 1) * HEAD_SIZE]


def stage_kernel(*refs):
    slabs = (len(refs) - 6) // 2
    own, other = refs[:slabs], refs[slabs : 2 * slabs]
    cos_ref, sin_ref, k_ref, v_ref, ck_ref, cv_ref = refs[2 * slabs :]
    me = lax.axis_index("blk")
    chip, core = me // CORES, me % CORES
    rows = own[0].shape[0]
    for j in range(slabs):
        for piece, side in ((own[j], core), (other[j], 1 - core)):
            at = pl.multiple_of(((chip ^ j) * CORES + side) * rows, rows)
            here = pl.ds(at, rows)
            k_ref[here] = rotate(lanes(piece, 0), cos_ref[here], sin_ref[here])
            v_ref[here] = lanes(piece, 1)
            ck_ref[here] = lanes(piece, 2)
            cv_ref[here] = lanes(piece, 3)


def attend_kernel(group, own_half, *refs):
    queries, rest = refs[:-9], refs[-9:]
    k_ref, v_ref, ck_ref, cv_ref, cos_ref, sin_ref, ctx_ref, out_ref, q_s = rest
    slabs = len(queries)
    me = lax.axis_index("blk")
    chip, core = me // CORES, me % CORES
    rows = queries[0].shape[0]
    span = rows * CORES
    half = lax.axis_index("heads") if own_half else 1 - lax.axis_index("heads")

    def turn(j):
        source = chip ^ j
        here = pl.ds(pl.multiple_of(source * span + core * rows, rows), rows)
        for h in range(group):
            at = pl.multiple_of((source * group + h) * rows, rows)
            q_s[pl.ds(at, rows)] = rotate(lanes(queries[j], h), cos_ref[here], sin_ref[here])

    for j in range(slabs):
        pl.when((chip ^ j) // (slabs // 2) == half)(functools.partial(turn, j))

    scale = math.log2(math.e) / math.sqrt(HEAD_SIZE)
    height = group * rows
    total_rows = slabs * span
    cached_ok = lax.broadcasted_iota(jnp.int32, (1, total_rows), 1) < ctx_ref[0]
    cached_bias = jnp.where(cached_ok, 0.0, NEG_FILL).astype(jnp.float32)
    row = lax.broadcasted_iota(jnp.int32, (height, span), 0) % rows + core * rows
    col = lax.broadcasted_iota(jnp.int32, (height, span), 1)
    diagonal = col <= row

    def scores_of(q, keys):
        dot = lax.dot_general(q, keys, (((1,), (1,)), ((), ())), preferred_element_type=jnp.float32)
        return dot * scale

    def attend(blocks):
        for n, block in enumerate(blocks):
            q = q_s[block * height : (block + 1) * height]
            begin, end = block * span, (block + 1) * span
            parts = [
                (scores_of(q, ck_ref[...]) + cached_bias, cv_ref[...]),
                (jnp.where(diagonal, scores_of(q, k_ref[begin:end]), NEG_FILL), v_ref[begin:end]),
            ]
            if block:
                parts.append((scores_of(q, k_ref[:begin]), v_ref[:begin]))
            top = functools.reduce(jnp.maximum, [jnp.max(scores, axis=1, keepdims=True) for scores, _ in parts])
            total, summed = 0.0, 0.0
            for scores, values in parts:
                exp_scores = jnp.exp2(scores - top)
                total = total + jnp.sum(exp_scores, axis=1, keepdims=True)
                summed = summed + jnp.dot(
                    exp_scores.astype(jnp.bfloat16), values, preferred_element_type=jnp.float32
                )
            result = (summed / total).astype(jnp.bfloat16)
            for h in range(group):
                out_ref[n, :, h * HEAD_SIZE : (h + 1) * HEAD_SIZE] = result[h * rows : (h + 1) * rows]

    for value in range(2):
        blocks = tuple(range(value * slabs // 2, (value + 1) * slabs // 2))
        pl.when(half == value)(functools.partial(attend, blocks))


def project_kernel(distances, final, column, w_ref, *refs):
    pieces = len(distances)
    own, other, added = refs[:pieces], refs[pieces : 2 * pieces], refs[2 * pieces :]
    added, scratch = (added[:-4], added[-4:]) if final else (added[:-2], added[-2:])
    out_ref, rows_s = scratch[:2]
    me = lax.axis_index("blk")
    chip, core = me // CORES, me % CORES
    blocks, rows, width = own[0].shape
    apart = pieces < w_ref.shape[1] // width
    for j in range(pieces):
        at = 0 if apart else pl.multiple_of((chip ^ distances[j]) * width, HEAD_SIZE)
        for piece, side in ((own[j], core), (other[j], 1 - core)):
            for n in range(blocks):
                to = pl.multiple_of((n * CORES + side) * rows, rows)
                rows_s[j if apart else 0, pl.ds(to, rows), pl.ds(at, width)] = piece[n]

    def dot(a, b):
        return lax.dot_general(a, b, (((1,), (1,)), ((), ())), preferred_element_type=jnp.float32)

    def share(lines):
        if apart:
            total = None
            for j, distance in enumerate(distances):
                at = pl.multiple_of((chip ^ distance) * width, HEAD_SIZE)
                product = dot(w_ref[lines, pl.ds(at, width)], rows_s[j])
                total = product if total is None else total + product
        else:
            total = dot(w_ref[lines], rows_s[0])
        for ref in added:
            total = total + ref[lines, column : column + total.shape[1]].astype(jnp.float32)
        return total

    features = w_ref.shape[0]
    if not final:
        out_ref[...] = share(slice(0, features)).astype(out_ref.dtype)
        return
    staged, sem = scratch[2:]
    copies = []
    for n in range(2):
        lines = slice(n * features // 2, (n + 1) * features // 2)
        staged[lines] = share(lines).astype(out_ref.dtype)
        copies.append(pltpu.make_async_copy(staged.at[lines], out_ref.at[lines], sem.at[n]))
        copies[-1].start()
    for copy in copies:
        copy.wait()


def head_sharded(chips, span_q, span_k, span_values, cached_keys, cached_values, out_weight, ctx_len, span_start):
    rows = span_q.shape[0]
    group = span_q.shape[1] // span_k.shape[1]
    features = out_weight.shape[0]
    devices = chips * CORES
    total_rows = devices * rows
    width = group * HEAD_SIZE

    def along(j):
        return [(b, b ^ (CORES * j)) for b in range(devices)]

    partner = [(b, b ^ 1) for b in range(devices)]
    across = [(0, 1), (1, 0)]

    keyed = pack(KROOM, chips, (span_k, span_values, cached_keys, cached_values))[0]
    asked = pack(QROOM, chips, (span_q,))[0]
    half_dim = HEAD_SIZE // 2
    inverse = ROPE_BASE ** (-(jnp.arange(half_dim, dtype=jnp.float32) * 2.0 / HEAD_SIZE))
    positions = span_start[0] + jnp.arange(total_rows, dtype=jnp.int32)
    angles = positions.astype(jnp.float32)[:, None] * inverse[None, :]
    cosine, sine = jnp.cos(angles), jnp.sin(angles)
    cosine = jnp.concatenate([cosine, cosine], axis=1)
    sine = jnp.concatenate([-sine, sine], axis=1)

    keys = [keyed[0]] + [lax.ppermute(keyed[j], "blk", along(j)) for j in range(1, chips)]
    queries = [asked[0]] + [lax.ppermute(asked[j], "blk", along(j)) for j in range(1, chips)]
    keys[1], cosine, sine = lax.optimization_barrier((keys[1], cosine, sine))
    keys[0], cosine, sine = lax.optimization_barrier((keys[0], cosine, sine))
    swapped = [lax.ppermute(x, "blk", partner) for x in keys]
    half_chips = chips // 2

    lined = jax.ShapeDtypeStruct((total_rows, HEAD_SIZE), jnp.bfloat16)
    staged = pl.pallas_call(
        stage_kernel,
        out_shape=[lined] * 4,
        in_specs=[whole()] * (2 * chips + 2),
        out_specs=[whole()] * 4,
        name="stage",
        compiler_params=room(8),
        cost_estimate=pl.CostEstimate(flops=1_000_000, bytes_accessed=1_000_000, transcendentals=0),
    )(*keys, *swapped, cosine, sine)

    def attend(own_half):
        return pl.pallas_call(
            functools.partial(attend_kernel, group, own_half),
            out_shape=jax.ShapeDtypeStruct((half_chips, rows, width), jnp.bfloat16),
            in_specs=[whole()] * (chips + 6) + [whole(pltpu.SMEM)],
            out_specs=whole(),
            scratch_shapes=[pltpu.VMEM((chips * group * rows, HEAD_SIZE), jnp.bfloat16)],
            name="attend",
            compiler_params=room(12),
            cost_estimate=pl.CostEstimate(flops=400_000_000, bytes_accessed=1_000_000, transcendentals=600_000),
        )(*queries, *staged, cosine, sine, ctx_len)

    def project(distances, pieces, others, *added, dtype=jnp.bfloat16, final=False, column=0):
        count = pieces[0].shape[0] * CORES * rows
        apart = len(pieces) < chips
        scratch = [pltpu.VMEM((len(pieces), count, width) if apart else (1, count, chips * width), jnp.bfloat16)]
        if final:
            scratch += [pltpu.VMEM((features, count), dtype), pltpu.SemaphoreType.DMA((2,))]
        return pl.pallas_call(
            functools.partial(project_kernel, distances, final, column),
            out_shape=jax.ShapeDtypeStruct((features, count), dtype),
            in_specs=[whole()] * (1 + 2 * len(pieces) + len(added)),
            out_specs=whole(pl.ANY if final else pltpu.VMEM),
            scratch_shapes=scratch,
            name="project",
            compiler_params=room(12),
            cost_estimate=pl.CostEstimate(
                flops=2 * features * width * count * len(pieces), bytes_accessed=1_000_000, transcendentals=0
            ),
        )(out_weight, *pieces, *others, *added)

    def swap(pieces):
        return [lax.ppermute(piece, "blk", partner) for piece in pieces]

    sent = attend(False)
    far = lax.ppermute(sent, "blk", along(2))
    near = lax.ppermute(sent, "blk", along(1))
    pieces = [sent, near, far]
    others = swap(pieces)
    early = project((0,), pieces[:1], others[:1], dtype=jnp.float32)
    early = project((1, 2), pieces[1:], others[1:], early, dtype=jnp.float32)
    received = []
    for n in range(half_chips):
        relayed = lax.ppermute(far[n : n + 1], "blk", along(1))
        other = lax.ppermute(relayed, "blk", partner)
        partial = project((3,), [relayed], [other], early, column=n * CORES * rows)
        received.append(lax.ppermute(partial, "heads", across))
    kept = attend(True)
    pieces = [kept] + [lax.ppermute(kept, "blk", along(j)) for j in (1, 2, 3)]
    others = swap(pieces)
    early = project((0,), pieces[:1], others[:1], dtype=jnp.float32)
    received = jnp.concatenate(received, axis=1)
    return project((1, 2, 3), pieces[1:], others[1:], early, received, final=True)


def rotary(inputs, positions):
    row_count = inputs.shape[0]
    head_count = inputs.shape[1] // HEAD_SIZE
    floats = inputs.astype(jnp.float32).reshape(row_count, head_count, HEAD_SIZE)
    half_dim = HEAD_SIZE // 2
    inverse = ROPE_BASE ** (-(jnp.arange(half_dim, dtype=jnp.float32) * 2.0 / HEAD_SIZE))
    angles = positions.astype(jnp.float32)[:, None] * inverse[None, :]
    cosine = jnp.cos(angles)[:, None, :]
    sine_val = jnp.sin(angles)[:, None, :]
    first_half = floats[..., :half_dim]
    second_half = floats[..., half_dim:]
    rotated = jnp.concatenate(
        [
            first_half * cosine - second_half * sine_val,
            second_half * cosine + first_half * sine_val,
        ],
        axis=-1,
    )
    return rotated.reshape(row_count, head_count * HEAD_SIZE).astype(jnp.bfloat16)


def token_sharded(span_q, span_k, span_values, cached_keys, cached_values, out_weight, ctx_len, span_start):
    own_index = lax.axis_index("blk")
    local_rows = span_q.shape[0]
    stored_rows = cached_keys.shape[0]
    key_heads = span_k.shape[1] // HEAD_SIZE
    queries_per_group = span_q.shape[1] // span_k.shape[1]
    query_index = own_index * local_rows + jnp.arange(local_rows, dtype=jnp.int32)
    positions = span_start[0] + query_index
    query_rows = rotary(span_q, positions).reshape(
        local_rows, key_heads, queries_per_group, HEAD_SIZE
    )
    new_keys = rotary(span_k, positions)
    cache_limit = ctx_len[0]
    initial = (
        jnp.full((key_heads, queries_per_group, local_rows), NEG_FILL, jnp.float32),
        jnp.zeros((key_heads, queries_per_group, local_rows), jnp.float32),
        jnp.zeros((key_heads, queries_per_group, local_rows, HEAD_SIZE), jnp.float32),
    )
    packed = jnp.concatenate(
        [
            jnp.concatenate([cached_keys, cached_values], axis=1),
            jnp.concatenate([new_keys, span_values], axis=1),
        ],
        axis=0,
    )
    shard_len = stored_rows + local_rows
    key_width = key_heads * HEAD_SIZE
    block_limit = 2560
    running = initial
    piece = lax.all_gather(packed, "blk", axis=0, tiled=True)
    start = jnp.int32(0)
    total_rows = piece.shape[0]
    for row_offset in range(0, total_rows, block_limit):
        row_block = piece[row_offset : row_offset + block_limit]
        row_index = start + row_offset + jnp.arange(row_block.shape[0], dtype=jnp.int32)
        shard_id = row_index // shard_len
        within = row_index % shard_len
        is_cache = within < stored_rows
        cache_pos = shard_id * stored_rows + within
        span_pos = shard_id * local_rows + within - stored_rows
        visible = jnp.where(
            is_cache[None, :],
            (cache_pos < cache_limit)[None, :],
            span_pos[None, :] <= query_index[:, None],
        )
        key_block = row_block[:, :key_width].reshape(-1, key_heads, HEAD_SIZE)
        value_block = row_block[:, key_width:].reshape(-1, key_heads, HEAD_SIZE)
        scores = jnp.einsum(
            "qgkd,tgd->gkqt", query_rows, key_block, preferred_element_type=jnp.float32
        ) / math.sqrt(HEAD_SIZE)
        scores = jnp.where(visible[None, None], scores, NEG_FILL)
        attend_largest, attend_denominator, attend_weighted = running
        new_largest = jnp.maximum(attend_largest, jnp.max(scores, axis=-1))
        shrink = jnp.exp(attend_largest - new_largest)
        exp_scores = jnp.exp(scores - new_largest[..., None])
        attend_denominator = attend_denominator * shrink + jnp.sum(exp_scores, axis=-1)
        product = jnp.einsum(
            "gkqt,tgd->gkqd",
            exp_scores.astype(jnp.bfloat16),
            value_block,
            preferred_element_type=jnp.float32,
        )
        attend_weighted = attend_weighted * shrink[..., None] + product
        running = (new_largest, attend_denominator, attend_weighted)
    _, denominator, weighted = running
    normalized = weighted / denominator[..., None]
    attended = (
        jnp.transpose(normalized, (2, 0, 1, 3))
        .reshape(local_rows, key_heads * queries_per_group * HEAD_SIZE)
        .astype(jnp.bfloat16)
    )
    partial_value = lax.dot_general(
        out_weight,
        lax.all_gather(attended, "blk", axis=0, tiled=True),
        (((1,), (1,)), ((), ())),
        preferred_element_type=jnp.float32,
    )
    summed = lax.psum_scatter(
        partial_value.astype(jnp.bfloat16), "heads", scatter_dimension=1, tiled=True
    )
    return summed


def local(blk, heads, span_q, span_k, *others):
    chips = blk // CORES
    key_heads = span_k.shape[1] // HEAD_SIZE
    if by_head(blk, heads, key_heads):
        return head_sharded(chips, span_q, span_k, *others)
    return token_sharded(span_q, span_k, *others)


def by_head(blk, heads, key_heads):
    return blk == CORES * key_heads and key_heads == 4 and heads == 2


def solution(mesh):
    placed = (
        P(("groups", "blk"), "heads"),
        P(("groups", "blk"), "heads"),
        P(("groups", "blk"), "heads"),
        P(("groups", "blk"), "heads"),
        P(("groups", "blk"), "heads"),
        P("blk", "heads"),
        P("groups"),
        P("groups"),
    )
    return jax.shard_map(
        functools.partial(local, mesh.shape["blk"], mesh.shape["heads"]),
        mesh=mesh,
        in_specs=placed,
        out_specs=P("blk", ("groups", "heads")),
        check_vma=False,
    )
```

```python
import functools
import math

import jax
import jax.numpy as jnp
from jax import lax
from jax.experimental import pallas as pl
from jax.experimental.pallas import tpu as pltpu
from jax.sharding import PartitionSpec as P


HEAD_SIZE = 128
CORES = 2


ROPE_BASE = 1000000.0
NEG_FILL = -1e30


def whole(space=pltpu.VMEM):
    return pl.BlockSpec(memory_space=space)


def room(mib):
    return pltpu.CompilerParams(vmem_limit_bytes=mib * 1024 * 1024)


KROOM = 54950
QROOM = 54800


def pack_kernel(chips, groups, *refs):
    total = sum(groups)
    arrays, refs = refs[:total], refs[total:]
    chip = lax.axis_index("blk") // CORES
    order = list(reversed(range(chips)))
    taken, given = {}, []
    for g, size in enumerate(groups):
        outs, held, in_sem = refs[g * chips : (g + 1) * chips], refs[g - 3 * len(groups)], refs[g - 2 * len(groups)]
        for j in order:
            taken[g, j] = []
            to = 0
            for n, ref in enumerate(arrays[sum(groups[:g]) : sum(groups[:g]) + size]):
                count = ref.shape[1] // chips
                at = pl.multiple_of((chip ^ j) * count, HEAD_SIZE)
                taken[g, j].append(
                    pltpu.make_async_copy(
                        ref.at[:, pl.ds(at, count)], held.at[j, :, pl.ds(to, count)], in_sem.at[j, n]
                    )
                )
                taken[g, j][-1].start()
                to += count
    for g in range(len(groups)):
        outs, held, out_sem = refs[g * chips : (g + 1) * chips], refs[g - 3 * len(groups)], refs[g - len(groups)]
        for j in order:
            for copy in taken[g, j]:
                copy.wait()
            given.append(pltpu.make_async_copy(held.at[j], outs[j], out_sem.at[j]))
            given[-1].start()
    for copy in given:
        copy.wait()


def pack(kib, chips, *groups):
    slabs = [(group[0].shape[0], sum(x.shape[1] for x in group) // chips) for group in groups]
    out = pl.pallas_call(
        functools.partial(pack_kernel, chips, [len(group) for group in groups]),
        out_shape=[jax.ShapeDtypeStruct(slab, jnp.bfloat16) for slab in slabs for _ in range(chips)],
        in_specs=[whole(pl.ANY) for group in groups for _ in group],
        out_specs=[whole(pl.ANY) for _ in slabs for _ in range(chips)],
        scratch_shapes=[pltpu.VMEM((chips, *slab), jnp.bfloat16) for slab in slabs]
        + [pltpu.SemaphoreType.DMA((chips, len(group))) for group in groups]
        + [pltpu.SemaphoreType.DMA((chips,)) for _ in groups],
        compiler_params=pltpu.CompilerParams(vmem_limit_bytes=kib * 1024),
    )(*(x for group in groups for x in group))
    return [out[g * chips : (g + 1) * chips] for g in range(len(groups))]


def rotate(x, cosine, sine):
    x = x.astype(jnp.float32)
    turned = pltpu.roll(x, HEAD_SIZE // 2, 1)
    return (x * cosine + turned * sine).astype(jnp.bfloat16)


def lanes(piece, n):
    return piece[:, n * HEAD_SIZE : (n + 1) * HEAD_SIZE]


def stage_kernel(*refs):
    slabs = (len(refs) - 4) // 2
    own, other = refs[:slabs], refs[slabs : 2 * slabs]
    cos_ref, sin_ref, k_ref, v_ref = refs[2 * slabs :]
    me = lax.axis_index("blk")
    chip, core = me // CORES, me % CORES
    rows = own[0].shape[0]
    for j in range(slabs):
        for piece, side in ((own[j], core), (other[j], 1 - core)):
            at = pl.multiple_of(((chip ^ j) * CORES + side) * rows, rows)
            here = pl.ds(at, rows)
            new = pl.ds(pl.multiple_of(cos_ref.shape[0] + at, rows), rows)
            k_ref[new] = rotate(lanes(piece, 0), cos_ref[here], sin_ref[here])
            v_ref[new] = lanes(piece, 1)
            k_ref[here] = lanes(piece, 2)
            v_ref[here] = lanes(piece, 3)


def attend_kernel(group, own_half, *refs):
    queries, rest = refs[:-7], refs[-7:]
    k_ref, v_ref, cos_ref, sin_ref, ctx_ref, out_ref, q_s = rest
    slabs = len(queries)
    me = lax.axis_index("blk")
    chip, core = me // CORES, me % CORES
    rows = queries[0].shape[0]
    span = rows * CORES
    half = lax.axis_index("heads") if own_half else 1 - lax.axis_index("heads")

    def turn(j):
        source = chip ^ j
        here = pl.ds(pl.multiple_of(source * span + core * rows, rows), rows)
        for h in range(group):
            at = pl.multiple_of((source * group + h) * rows, rows)
            q_s[pl.ds(at, rows)] = rotate(lanes(queries[j], h), cos_ref[here], sin_ref[here])

    for j in range(slabs):
        pl.when((chip ^ j) // (slabs // 2) == half)(functools.partial(turn, j))

    scale = math.log2(math.e) / math.sqrt(HEAD_SIZE)
    height = group * rows
    total_rows = slabs * span
    place = lax.broadcasted_iota(jnp.int32, (1, 2 * total_rows), 1)
    hidden = jnp.logical_and(place >= ctx_ref[0], place < total_rows)
    bias = jnp.where(hidden, NEG_FILL, 0.0).astype(jnp.float32)
    row = lax.broadcasted_iota(jnp.int32, (height, span), 0) % rows + core * rows
    col = lax.broadcasted_iota(jnp.int32, (height, span), 1)
    diagonal = col <= row

    def scores_of(q, keys):
        dot = lax.dot_general(q, keys, (((1,), (1,)), ((), ())), preferred_element_type=jnp.float32)
        return dot * scale

    def attend(blocks):
        for n, block in enumerate(blocks):
            q = q_s[block * height : (block + 1) * height]
            begin, end = total_rows + block * span, total_rows + (block + 1) * span
            parts = [
                (scores_of(q, k_ref[:begin]) + bias[:, :begin], v_ref[:begin]),
                (jnp.where(diagonal, scores_of(q, k_ref[begin:end]), NEG_FILL), v_ref[begin:end]),
            ]
            top = functools.reduce(jnp.maximum, [jnp.max(scores, axis=1, keepdims=True) for scores, _ in parts])
            total, summed = 0.0, 0.0
            for scores, values in parts:
                exp_scores = jnp.exp2(scores - top)
                total = total + jnp.sum(exp_scores, axis=1, keepdims=True)
                summed = summed + jnp.dot(
                    exp_scores.astype(jnp.bfloat16), values, preferred_element_type=jnp.float32
                )
            result = (summed / total).astype(jnp.bfloat16)
            for h in range(group):
                out_ref[n, :, h * HEAD_SIZE : (h + 1) * HEAD_SIZE] = result[h * rows : (h + 1) * rows]

    for value in range(2):
        blocks = tuple(range(value * slabs // 2, (value + 1) * slabs // 2))
        pl.when(half == value)(functools.partial(attend, blocks))


def project_kernel(distances, final, column, w_ref, *refs):
    pieces = len(distances)
    own, other, added = refs[:pieces], refs[pieces : 2 * pieces], refs[2 * pieces :]
    added, scratch = (added[:-4], added[-4:]) if final else (added[:-2], added[-2:])
    out_ref, rows_s = scratch[:2]
    me = lax.axis_index("blk")
    chip, core = me // CORES, me % CORES
    blocks, rows, width = own[0].shape
    apart = pieces < w_ref.shape[1] // width
    for j in range(pieces):
        at = 0 if apart else pl.multiple_of((chip ^ distances[j]) * width, HEAD_SIZE)
        for piece, side in ((own[j], core), (other[j], 1 - core)):
            for n in range(blocks):
                to = pl.multiple_of((n * CORES + side) * rows, rows)
                rows_s[j if apart else 0, pl.ds(to, rows), pl.ds(at, width)] = piece[n]

    def dot(a, b):
        return lax.dot_general(a, b, (((1,), (1,)), ((), ())), preferred_element_type=jnp.float32)

    def share(lines):
        if apart:
            total = None
            for j, distance in enumerate(distances):
                at = pl.multiple_of((chip ^ distance) * width, HEAD_SIZE)
                product = dot(w_ref[lines, pl.ds(at, width)], rows_s[j])
                total = product if total is None else total + product
        else:
            total = dot(w_ref[lines], rows_s[0])
        for ref in added:
            total = total + ref[lines, column : column + total.shape[1]].astype(jnp.float32)
        return total

    features = w_ref.shape[0]
    if not final:
        out_ref[...] = share(slice(0, features)).astype(out_ref.dtype)
        return
    staged, sem = scratch[2:]
    copies = []
    for n in range(2):
        lines = slice(n * features // 2, (n + 1) * features // 2)
        staged[lines] = share(lines).astype(out_ref.dtype)
        copies.append(pltpu.make_async_copy(staged.at[lines], out_ref.at[lines], sem.at[n]))
        copies[-1].start()
    for copy in copies:
        copy.wait()


def head_sharded(chips, span_q, span_k, span_values, cached_keys, cached_values, out_weight, ctx_len, span_start):
    rows = span_q.shape[0]
    group = span_q.shape[1] // span_k.shape[1]
    features = out_weight.shape[0]
    devices = chips * CORES
    total_rows = devices * rows
    width = group * HEAD_SIZE

    def along(j):
        return [(b, b ^ (CORES * j)) for b in range(devices)]

    partner = [(b, b ^ 1) for b in range(devices)]
    across = [(0, 1), (1, 0)]

    keyed = pack(KROOM, chips, (span_k, span_values, cached_keys, cached_values))[0]
    asked = pack(QROOM, chips, (span_q,))[0]
    half_dim = HEAD_SIZE // 2
    inverse = ROPE_BASE ** (-(jnp.arange(half_dim, dtype=jnp.float32) * 2.0 / HEAD_SIZE))
    positions = span_start[0] + jnp.arange(total_rows, dtype=jnp.int32)
    angles = positions.astype(jnp.float32)[:, None] * inverse[None, :]
    cosine, sine = jnp.cos(angles), jnp.sin(angles)
    cosine = jnp.concatenate([cosine, cosine], axis=1)
    sine = jnp.concatenate([-sine, sine], axis=1)

    keys = [keyed[0]] + [lax.ppermute(keyed[j], "blk", along(j)) for j in range(1, chips)]
    queries = [asked[0]] + [lax.ppermute(asked[j], "blk", along(j)) for j in range(1, chips)]
    keys[1], cosine, sine = lax.optimization_barrier((keys[1], cosine, sine))
    keys[0], cosine, sine = lax.optimization_barrier((keys[0], cosine, sine))
    swapped = [lax.ppermute(x, "blk", partner) for x in keys]
    half_chips = chips // 2

    lined = jax.ShapeDtypeStruct((2 * total_rows, HEAD_SIZE), jnp.bfloat16)
    staged = pl.pallas_call(
        stage_kernel,
        out_shape=[lined] * 2,
        in_specs=[whole()] * (2 * chips + 2),
        out_specs=[whole()] * 2,
        name="stage",
        compiler_params=room(8),
        cost_estimate=pl.CostEstimate(flops=1_000_000, bytes_accessed=1_000_000, transcendentals=0),
    )(*keys, *swapped, cosine, sine)

    def attend(own_half):
        return pl.pallas_call(
            functools.partial(attend_kernel, group, own_half),
            out_shape=jax.ShapeDtypeStruct((half_chips, rows, width), jnp.bfloat16),
            in_specs=[whole()] * (chips + 4) + [whole(pltpu.SMEM)],
            out_specs=whole(),
            scratch_shapes=[pltpu.VMEM((chips * group * rows, HEAD_SIZE), jnp.bfloat16)],
            name="attend",
            compiler_params=room(12),
            cost_estimate=pl.CostEstimate(flops=400_000_000, bytes_accessed=1_000_000, transcendentals=600_000),
        )(*queries, *staged, cosine, sine, ctx_len)

    def project(distances, pieces, others, *added, dtype=jnp.bfloat16, final=False, column=0):
        count = pieces[0].shape[0] * CORES * rows
        apart = len(pieces) < chips
        scratch = [pltpu.VMEM((len(pieces), count, width) if apart else (1, count, chips * width), jnp.bfloat16)]
        if final:
            scratch += [pltpu.VMEM((features, count), dtype), pltpu.SemaphoreType.DMA((2,))]
        return pl.pallas_call(
            functools.partial(project_kernel, distances, final, column),
            out_shape=jax.ShapeDtypeStruct((features, count), dtype),
            in_specs=[whole()] * (1 + 2 * len(pieces) + len(added)),
            out_specs=whole(pl.ANY if final else pltpu.VMEM),
            scratch_shapes=scratch,
            name="project",
            compiler_params=room(12),
            cost_estimate=pl.CostEstimate(
                flops=2 * features * width * count * len(pieces), bytes_accessed=1_000_000, transcendentals=0
            ),
        )(out_weight, *pieces, *others, *added)

    def swap(pieces):
        return [lax.ppermute(piece, "blk", partner) for piece in pieces]

    sent = attend(False)
    far = lax.ppermute(sent, "blk", along(2))
    near = lax.ppermute(sent, "blk", along(1))
    pieces = [sent, near, far]
    others = swap(pieces)
    early = project((0,), pieces[:1], others[:1], dtype=jnp.float32)
    early = project((1, 2), pieces[1:], others[1:], early, dtype=jnp.float32)
    received = []
    for n in range(half_chips):
        relayed = lax.ppermute(far[n : n + 1], "blk", along(1))
        other = lax.ppermute(relayed, "blk", partner)
        partial = project((3,), [relayed], [other], early, column=n * CORES * rows)
        received.append(lax.ppermute(partial, "heads", across))
    kept = attend(True)
    pieces = [kept] + [lax.ppermute(kept, "blk", along(j)) for j in (1, 2, 3)]
    others = swap(pieces)
    early = project((0,), pieces[:1], others[:1], dtype=jnp.float32)
    received = jnp.concatenate(received, axis=1)
    return project((1, 2, 3), pieces[1:], others[1:], early, received, final=True)


def rotary(inputs, positions):
    row_count = inputs.shape[0]
    head_count = inputs.shape[1] // HEAD_SIZE
    floats = inputs.astype(jnp.float32).reshape(row_count, head_count, HEAD_SIZE)
    half_dim = HEAD_SIZE // 2
    inverse = ROPE_BASE ** (-(jnp.arange(half_dim, dtype=jnp.float32) * 2.0 / HEAD_SIZE))
    angles = positions.astype(jnp.float32)[:, None] * inverse[None, :]
    cosine = jnp.cos(angles)[:, None, :]
    sine_val = jnp.sin(angles)[:, None, :]
    first_half = floats[..., :half_dim]
    second_half = floats[..., half_dim:]
    rotated = jnp.concatenate(
        [
            first_half * cosine - second_half * sine_val,
            second_half * cosine + first_half * sine_val,
        ],
        axis=-1,
    )
    return rotated.reshape(row_count, head_count * HEAD_SIZE).astype(jnp.bfloat16)


def token_sharded(span_q, span_k, span_values, cached_keys, cached_values, out_weight, ctx_len, span_start):
    own_index = lax.axis_index("blk")
    local_rows = span_q.shape[0]
    stored_rows = cached_keys.shape[0]
    key_heads = span_k.shape[1] // HEAD_SIZE
    queries_per_group = span_q.shape[1] // span_k.shape[1]
    query_index = own_index * local_rows + jnp.arange(local_rows, dtype=jnp.int32)
    positions = span_start[0] + query_index
    query_rows = rotary(span_q, positions).reshape(
        local_rows, key_heads, queries_per_group, HEAD_SIZE
    )
    new_keys = rotary(span_k, positions)
    cache_limit = ctx_len[0]
    initial = (
        jnp.full((key_heads, queries_per_group, local_rows), NEG_FILL, jnp.float32),
        jnp.zeros((key_heads, queries_per_group, local_rows), jnp.float32),
        jnp.zeros((key_heads, queries_per_group, local_rows, HEAD_SIZE), jnp.float32),
    )
    packed = jnp.concatenate(
        [
            jnp.concatenate([cached_keys, cached_values], axis=1),
            jnp.concatenate([new_keys, span_values], axis=1),
        ],
        axis=0,
    )
    shard_len = stored_rows + local_rows
    key_width = key_heads * HEAD_SIZE
    block_limit = 2560
    running = initial
    piece = lax.all_gather(packed, "blk", axis=0, tiled=True)
    start = jnp.int32(0)
    total_rows = piece.shape[0]
    for row_offset in range(0, total_rows, block_limit):
        row_block = piece[row_offset : row_offset + block_limit]
        row_index = start + row_offset + jnp.arange(row_block.shape[0], dtype=jnp.int32)
        shard_id = row_index // shard_len
        within = row_index % shard_len
        is_cache = within < stored_rows
        cache_pos = shard_id * stored_rows + within
        span_pos = shard_id * local_rows + within - stored_rows
        visible = jnp.where(
            is_cache[None, :],
            (cache_pos < cache_limit)[None, :],
            span_pos[None, :] <= query_index[:, None],
        )
        key_block = row_block[:, :key_width].reshape(-1, key_heads, HEAD_SIZE)
        value_block = row_block[:, key_width:].reshape(-1, key_heads, HEAD_SIZE)
        scores = jnp.einsum(
            "qgkd,tgd->gkqt", query_rows, key_block, preferred_element_type=jnp.float32
        ) / math.sqrt(HEAD_SIZE)
        scores = jnp.where(visible[None, None], scores, NEG_FILL)
        attend_largest, attend_denominator, attend_weighted = running
        new_largest = jnp.maximum(attend_largest, jnp.max(scores, axis=-1))
        shrink = jnp.exp(attend_largest - new_largest)
        exp_scores = jnp.exp(scores - new_largest[..., None])
        attend_denominator = attend_denominator * shrink + jnp.sum(exp_scores, axis=-1)
        product = jnp.einsum(
            "gkqt,tgd->gkqd",
            exp_scores.astype(jnp.bfloat16),
            value_block,
            preferred_element_type=jnp.float32,
        )
        attend_weighted = attend_weighted * shrink[..., None] + product
        running = (new_largest, attend_denominator, attend_weighted)
    _, denominator, weighted = running
    normalized = weighted / denominator[..., None]
    attended = (
        jnp.transpose(normalized, (2, 0, 1, 3))
        .reshape(local_rows, key_heads * queries_per_group * HEAD_SIZE)
        .astype(jnp.bfloat16)
    )
    partial_value = lax.dot_general(
        out_weight,
        lax.all_gather(attended, "blk", axis=0, tiled=True),
        (((1,), (1,)), ((), ())),
        preferred_element_type=jnp.float32,
    )
    summed = lax.psum_scatter(
        partial_value.astype(jnp.bfloat16), "heads", scatter_dimension=1, tiled=True
    )
    return summed


def local(blk, heads, span_q, span_k, *others):
    chips = blk // CORES
    key_heads = span_k.shape[1] // HEAD_SIZE
    if by_head(blk, heads, key_heads):
        return head_sharded(chips, span_q, span_k, *others)
    return token_sharded(span_q, span_k, *others)


def by_head(blk, heads, key_heads):
    return blk == CORES * key_heads and key_heads == 4 and heads == 2


def solution(mesh):
    placed = (
        P(("groups", "blk"), "heads"),
        P(("groups", "blk"), "heads"),
        P(("groups", "blk"), "heads"),
        P(("groups", "blk"), "heads"),
        P(("groups", "blk"), "heads"),
        P("blk", "heads"),
        P("groups"),
        P("groups"),
    )
    return jax.shard_map(
        functools.partial(local, mesh.shape["blk"], mesh.shape["heads"]),
        mesh=mesh,
        in_specs=placed,
        out_specs=P("blk", ("groups", "heads")),
        check_vma=False,
    )
```
